512 devices in a mesh: grp: 32 (over y, z_lo), tp: 16 (over z_hi, x, core).
Axes of the slice: x: 4, y: 4, z: 16 (z_hi: 2, z_lo: 8; z = z_hi * 8 + z_lo), core: 2. Of those that a mesh axis runs over, the one named last changes fastest.
Arguments:
- tokens: bfloat16 [65536, 1536], P(('grp', 'tp')), may hold values from -6 to 6
- attn_gain: float32 [1536], replicated, may hold values from 0.1 to 1.9
- ffn_gain: float32 [1536], replicated, may hold values from 0.1 to 1.9
- w_query: bfloat16 [1536, 1024], P(None, 'tp')
- key_value_weight: bfloat16 [1536, 1024], P(None, 'tp'), may hold values from -0.15625 to 0.15625
- w_out: bfloat16 [1024, 1536], P('tp'), may hold values from -0.1875 to 0.1875
- segment_ids: int32 [65536], P(('grp', 'tp')), may hold values from 0 to 65535, as said below
- expert_ids: int32 [65536, 2], P(('grp', 'tp')), may hold values from 0 to 7, all different within a row; in each aligned block of 128 rows (0 to 127, 128 to 255, ...) at most 48 rows name the same one
- route_weights: float32 [65536, 2], P(('grp', 'tp')), may hold values from 0.2 to 1
- w_gate: bfloat16 [1536, 4096], P(None, 'tp'), may hold values from -0.15625 to 0.15625
- w_up: bfloat16 [1536, 4096], P(None, 'tp'), may hold values from -0.15625 to 0.15625
- w_down: bfloat16 [4096, 1536], P('tp'), may hold values from -0.25 to 0.25
- page_table: int32 [32, 128], P('grp'), may hold values from 0 to 127, each once within a row
Outputs:
- hidden_out: bfloat16 [65536, 1536], P(('grp', 'tp'))
- kv_cache: bfloat16 [4096, 16, 1024], P(('grp', 'tp'))
The draws below stay inside these ranges and needn't reach their ends.
Inputs may be any that keep to these rules, and one draw needn't show every extreme that they name: `segment_ids`: each token's number is the stream position of its prompt's first token, so numbers never fall along the stream; a prompt covers at most 1024 tokens and some prompt exactly 1024; a prompt runs from every group into the next; the last token of the stream is a prompt of its own. `expert_ids`: in the tokens of one device no expert is named more than 48 times; in some device's tokens one expert is named exactly 48 times. `page_table`: each row names every page of the group once.
All inputs are finite; a program needn't handle non-finite values.
Results may differ from the reference program's by a relative error of at most 0.015.
The reference program's roundings to bfloat16 on the way count: a program that leaves them out, or rounds other values in their place, can miss the bound.
Values may be sent and summed in bfloat16 or wider, within the bound.
No kernel may reach another device: no remote copies, remote signals or barrier semaphores. Data moves between devices by JAX's collectives and lax.ppermute only.
A program may use at most 64 MiB of HBM per device.

```python
import math
import jax
import jax.numpy as jnp
import numpy as np
from jax import lax

MODEL_DIM = 1536
HEAD_SIZE = 64
HQ = 16
KEY_VALUE_HEADS = 8
EFF = 512
TOP = 2
PAGE = 16
TOK_DEV = 128
GROUP_TOKENS = 2048
TOKENS = 65536
PROMPT_LENGTH = 1024
EXPERTS = 8
CAP = 48
PAGES_G = 128
N_GRP = 32
N_TP = 16


def draw_w_query(key, part):
    shape = (MODEL_DIM, HQ * HEAD_SIZE)
    inner_key = jax.random.fold_in(key, 5)
    values = jax.random.normal(inner_key, shape, jnp.float32) / math.sqrt(MODEL_DIM)
    return values.astype(jnp.bfloat16)


def draw_segment_ids(key, part):
    groups = TOKENS // GROUP_TOKENS
    half_len = PROMPT_LENGTH // 2
    key_tail, key_head, key_extra = jax.random.split(jax.random.fold_in(key, 11), 3)
    tail_len = jax.random.randint(key_tail, (groups,), 1, half_len + 1)
    head_len = jax.random.randint(key_head, (groups,), 1, half_len + 1)
    tail_len = tail_len.at[0].set(half_len)
    head_len = head_len.at[1].set(half_len)
    group_index = jnp.arange(groups)
    first_cut = jnp.where(group_index > 0, head_len, 0)
    last_cut = jnp.where(group_index < groups - 1, GROUP_TOKENS - tail_len, GROUP_TOKENS)
    middle_cut = (first_cut + last_cut) // 2
    position = jnp.arange(GROUP_TOKENS)[None, :]
    starts = (position == first_cut[:, None]) | (position == middle_cut[:, None])
    starts = starts | (position == last_cut[:, None]) & (group_index[:, None] < groups - 1)
    extra = jax.random.randint(key_extra, (groups, GROUP_TOKENS), 0, 512) == 0
    inside = (position > first_cut[:, None]) & (position < last_cut[:, None])
    starts = starts | extra & inside
    flags = starts.reshape(-1)
    stream_pos = jnp.arange(TOKENS, dtype=jnp.int32)
    flags = flags | (stream_pos == TOKENS - 1)
    marked = jnp.where(flags, stream_pos, 0).astype(jnp.int32)
    return lax.cummax(marked, axis=0).astype(jnp.int32)


def steps_of(own_key, dims, cuts, least, high):
    def one(dim, parts):
        heights = jax.random.uniform(jax.random.fold_in(jax.random.fold_in(own_key, 6), dim), (parts,), jnp.float32, least / len(cuts), high / len(cuts))
        return jnp.repeat(jnp.exp(heights), dims[dim] // parts).reshape((-1,) + (1,) * (len(dims) - dim - 1))

    gain = one(*cuts[0])
    for cut in cuts[1:]:
        gain = gain * one(*cut)
    return gain


def assign_block(key, own, number, rows, count, top, bound, slope):
    order = jax.random.permutation(key, count)
    packed, ordinary = shares(count, rows * top, bound, slope, True), shares(count, rows * top, bound, slope, False)
    places = jnp.arange(count)

    def named(tallies, offset_by):
        used = int((tallies > 0).sum())
        fixed = max(1, used // 4)
        shifted = fixed + (places - fixed + offset_by * (used - fixed)) % max(1, count - fixed)
        return jnp.zeros((count,), jnp.int32).at[order[jnp.where(places < fixed, places, shifted)]].set(jnp.asarray(tallies, jnp.int32))

    tallies = jnp.where(number % 4 == 0, named(packed, number // 4), named(ordinary, number - number // 4 - 1))
    mixed = jax.random.permutation(jax.random.fold_in(own, 3), count)
    giver, receiver = mixed[0:count // 2 * 2:2], mixed[1:count // 2 * 2:2]
    margin = jnp.minimum(tallies[giver] - 1, bound - tallies[receiver]) // 2
    margin = jnp.where((giver == order[0]) | (receiver == order[0]) | (tallies[receiver] == 0), 0, jnp.maximum(margin, 0))
    shifted = jax.random.randint(jax.random.fold_in(own, 4), (count // 2,), 0, 1 << 20) % (margin + 1)
    tallies = tallies.at[giver].add(-shifted).at[receiver].add(shifted)
    labels = jnp.searchsorted(jnp.cumsum(tallies), jnp.arange(rows * top), side="right").astype(jnp.int32)
    listing = labels.reshape(top, rows).T
    listing = listing[jax.random.permutation(jax.random.fold_in(own, 1), rows)]
    offset_by = jax.random.randint(jax.random.fold_in(own, 2), (rows, 1), 0, top)
    return jnp.take_along_axis(listing, (jnp.arange(top)[None, :] + offset_by) % top, axis=1)


def shares(amount, total, bound, slope, full):
    loads = [(1 << 20) // math.isqrt(rank ** slope) + 1 for rank in range(1, amount + 1)]
    largest = bound if full else min(bound, max(-(-total // amount), total * loads[0] // sum(loads)))
    least = 1 if total - largest >= amount - 1 else 0
    given, spare = [largest] + [least] * (amount - 1), total - largest - least * (amount - 1)
    while spare > 0:
        free = [i for i in range(1, amount) if given[i] < largest] or [i for i in range(1, amount) if given[i] < bound]
        mass, remaining = sum([loads[i] for i in free]), spare
        for i in free:
            more = min(bound - given[i], max(1, remaining * loads[i] // mass), spare)
            given[i] = given[i] + more
            spare = spare - more
    return np.array(given)


def noise(own_key, extent, spread, bound, cuts=(), kind=jnp.bfloat16):
    values = spread * jax.random.normal(own_key, extent, jnp.float32)
    if cuts:
        values = values * steps_of(own_key, extent, cuts, -0.22, 0.18)
    return jnp.clip(values, -bound, bound).astype(kind)


def setup_inputs(seed: int = 0) -> dict:
    key_of = jax.random.split(jax.random.key(seed), 14)
    tokens = noise(key_of[0], (TOKENS, MODEL_DIM), 1.0, 6.0, ((0, 512),))
    attn_gain = jnp.clip(1.0 + 0.18 * jax.random.normal(key_of[1], (MODEL_DIM,), jnp.float32), 0.1, 1.9)
    ffn_gain = jnp.clip(1.0 + 0.18 * jax.random.normal(key_of[2], (MODEL_DIM,), jnp.float32), 0.1, 1.9)
    w_query = draw_w_query(jax.random.fold_in(key_of[13], 71), 0)
    key_value_weight = noise(key_of[4], (MODEL_DIM, 2 * KEY_VALUE_HEADS * HEAD_SIZE), MODEL_DIM ** -0.5, 0.15625, ((1, 16),))
    w_out = noise(key_of[5], (HQ * HEAD_SIZE, MODEL_DIM), (HQ * HEAD_SIZE) ** -0.5, 0.1875, ((0, 16),))
    segment_ids = draw_segment_ids(jax.random.fold_in(key_of[13], 71), 0)
    expert_ids_keys = jax.random.split(jax.random.fold_in(key_of[7], 1), TOKENS // TOK_DEV)
    expert_ids_turns = jax.random.permutation(jax.random.fold_in(key_of[7], 3), TOKENS // TOK_DEV)
    expert_ids = jax.vmap(lambda own, number: assign_block(jax.random.fold_in(key_of[7], 2), own, number, TOK_DEV, EXPERTS, TOP, CAP, 2))(expert_ids_keys, expert_ids_turns).reshape((TOKENS, TOP))
    route_weights = jnp.clip(0.2 + 0.8 * jax.random.uniform(key_of[8], (TOKENS, TOP), jnp.float32) ** steps_of(key_of[8], (TOKENS, TOP), ((0, 512),), -0.2, 0.2), 0.2, 1.0)
    w_gate = noise(key_of[9], (MODEL_DIM, EXPERTS * EFF), MODEL_DIM ** -0.5, 0.15625, ((1, 16),))
    w_up = noise(key_of[10], (MODEL_DIM, EXPERTS * EFF), MODEL_DIM ** -0.5, 0.15625, ((1, 16),))
    w_down = noise(key_of[11], (EXPERTS * EFF, MODEL_DIM), EFF ** -0.5, 0.25, ((0, 16),))
    page_table = jax.vmap(lambda own: jax.random.permutation(own, PAGES_G))(jax.random.split(key_of[12], N_GRP)).reshape((N_GRP, PAGES_G)).astype(jnp.int32)
    return {"tokens": tokens, "attn_gain": attn_gain, "ffn_gain": ffn_gain, "w_query": w_query, "key_value_weight": key_value_weight, "w_out": w_out, "segment_ids": segment_ids, "expert_ids": expert_ids, "route_weights": route_weights, "w_gate": w_gate, "w_up": w_up, "w_down": w_down, "page_table": page_table}


def rms_scale(row_data, gain_vec):
    values = row_data.astype(jnp.float32)
    inverse = lax.rsqrt(lax.optimization_barrier(jnp.mean(values * values, axis=-1, keepdims=True)) + 1e-05)
    return (values * inverse * gain_vec).astype(jnp.bfloat16)

def group_attention(items):
    query_grp, key_grp, value_grp, seg_grp, key_prev, value_prev, seg_prev = items
    key_cat = jnp.concatenate([key_prev, key_grp], 0)
    value_cat = jnp.concatenate([value_prev, value_grp], 0)
    key_cat = jnp.concatenate([key_cat, key_cat], 1)
    value_cat = jnp.concatenate([value_cat, value_cat], 1)
    seg_cat = jnp.concatenate([seg_prev, seg_grp], 0)
    block_rows = min(512, GROUP_TOKENS)
    key_span = PROMPT_LENGTH + block_rows

    def one_block(block_index):
        first_row = block_index * block_rows
        query_block = lax.dynamic_slice_in_dim(query_grp, first_row, block_rows, 0).astype(jnp.float32)
        seg_query = lax.dynamic_slice_in_dim(seg_grp, first_row, block_rows, 0)
        key_block = lax.dynamic_slice_in_dim(key_cat, first_row, key_span, 0).astype(jnp.float32)
        value_block = lax.dynamic_slice_in_dim(value_cat, first_row, key_span, 0).astype(jnp.float32)
        seg_keys = lax.dynamic_slice_in_dim(seg_cat, first_row, key_span, 0)
        key_pos = first_row - PROMPT_LENGTH + jnp.arange(key_span, dtype=jnp.int32)
        query_pos = first_row + jnp.arange(block_rows, dtype=jnp.int32)
        scores = jnp.einsum('qhd,khd->hqk', query_block, key_block) * 0.125
        allowed = (seg_query[:, None] == seg_keys[None, :]) & (key_pos[None, :] <= query_pos[:, None])
        scores = jnp.where(allowed[None], scores, -1e+30)
        row_max = lax.optimization_barrier(jnp.max(scores, axis=-1, keepdims=True))
        exponent = jnp.exp(scores - row_max)
        attention = (exponent / lax.optimization_barrier(jnp.sum(exponent, axis=-1, keepdims=True))).astype(jnp.bfloat16)
        result = jnp.einsum('hqk,khd->qhd', attention.astype(jnp.float32), value_block)
        return result.astype(jnp.bfloat16)
    blocks = lax.map(one_block, jnp.arange(GROUP_TOKENS // block_rows, dtype=jnp.int32))
    return blocks.reshape(GROUP_TOKENS, HQ * HEAD_SIZE)

def reference(tokens, attn_gain, ffn_gain, w_query, key_value_weight, w_out, segment_ids, expert_ids, route_weights, w_gate, w_up, w_down, page_table):
    normed_in = rms_scale(tokens, attn_gain)
    queries = jnp.dot(normed_in, w_query, preferred_element_type=jnp.float32).astype(jnp.bfloat16)
    key_value_pairs = jnp.dot(normed_in, key_value_weight, preferred_element_type=jnp.float32).astype(jnp.bfloat16)
    key_value_width = 2 * KEY_VALUE_HEADS * HEAD_SIZE
    page_blocks = key_value_pairs.reshape(N_GRP, PAGES_G, PAGE, key_value_width)
    group_index = jnp.arange(N_GRP, dtype=jnp.int32)[:, None]
    cache_pages = jnp.zeros_like(page_blocks).at[group_index, page_table].set(page_blocks)
    kv_cache = cache_pages.reshape(N_GRP * PAGES_G, PAGE, key_value_width)
    width_half = KEY_VALUE_HEADS * HEAD_SIZE
    every_key = key_value_pairs[:, :width_half].reshape(N_GRP, GROUP_TOKENS, KEY_VALUE_HEADS, HEAD_SIZE)
    every_value = key_value_pairs[:, width_half:].reshape(N_GRP, GROUP_TOKENS, KEY_VALUE_HEADS, HEAD_SIZE)
    query_all = queries.reshape(N_GRP, GROUP_TOKENS, HQ, HEAD_SIZE)
    seg_all = segment_ids.reshape(N_GRP, GROUP_TOKENS)
    empty_keys = jnp.zeros((1, PROMPT_LENGTH, KEY_VALUE_HEADS, HEAD_SIZE), jnp.bfloat16)
    key_prev = jnp.concatenate([empty_keys, every_key[:-1, GROUP_TOKENS - PROMPT_LENGTH:]], 0)
    value_prev = jnp.concatenate([empty_keys, every_value[:-1, GROUP_TOKENS - PROMPT_LENGTH:]], 0)
    seg_prev = jnp.concatenate([jnp.full((1, PROMPT_LENGTH), -1, jnp.int32), seg_all[:-1, GROUP_TOKENS - PROMPT_LENGTH:]], 0)
    attended = lax.map(group_attention, (query_all, every_key, every_value, seg_all, key_prev, value_prev, seg_prev))
    attended = attended.reshape(TOKENS, HQ * HEAD_SIZE)
    mid_state = (tokens.astype(jnp.float32) + jnp.dot(attended, w_out, preferred_element_type=jnp.float32)).astype(jnp.bfloat16)
    normed_mid = rms_scale(mid_state, ffn_gain)
    half_units = EFF // 2
    route_count = TOK_DEV * TOP

    def group_experts(items):
        row_data, choice_ids, choice_weights = items
        block_ids = choice_ids.reshape(N_TP, route_count)
        expert_range = jnp.arange(EXPERTS, dtype=jnp.int32)
        onehot = (block_ids[..., None] == expert_range[None, None, :]).astype(jnp.int32)
        earlier = jnp.cumsum(onehot, axis=1) - onehot
        slot_index = lax.optimization_barrier(jnp.sum(earlier * onehot, axis=-1))
        source_grid = jnp.broadcast_to(jnp.arange(N_TP, dtype=jnp.int32)[:, None], (N_TP, route_count))
        token_index = source_grid * TOK_DEV + jnp.arange(route_count, dtype=jnp.int32)[None, :] // TOP
        buffers = jnp.zeros((EXPERTS, N_TP, CAP, MODEL_DIM), jnp.bfloat16)
        buffers = buffers.at[block_ids, source_grid, slot_index].set(row_data[token_index])

        def one_expert(expert_index):
            inputs = buffers[expert_index].reshape(N_TP * CAP, MODEL_DIM)
            gate_cols = lax.dynamic_slice_in_dim(w_gate, expert_index * EFF, EFF, 1)
            up_cols = lax.dynamic_slice_in_dim(w_up, expert_index * EFF, EFF, 1)
            down_rows = lax.dynamic_slice_in_dim(w_down, expert_index * EFF, EFF, 0)
            results = []
            for half_index in range(2):
                low_col = half_index * half_units
                gate_act = jnp.dot(inputs, gate_cols[:, low_col:low_col + half_units], preferred_element_type=jnp.float32)
                up_act = jnp.dot(inputs, up_cols[:, low_col:low_col + half_units], preferred_element_type=jnp.float32)
                activated = (jax.nn.silu(gate_act) * up_act).astype(jnp.bfloat16)
                half_out = jnp.dot(activated, down_rows[low_col:low_col + half_units], preferred_element_type=jnp.float32).astype(jnp.bfloat16)
                half_out = lax.optimization_barrier(half_out)
                results.append(half_out.astype(jnp.float32))
            return (results[0] + results[1]).reshape(N_TP, CAP, MODEL_DIM)
        expert_out = lax.map(one_expert, jnp.arange(EXPERTS, dtype=jnp.int32))
        picked = expert_out[block_ids, source_grid, slot_index].reshape(GROUP_TOKENS, TOP, MODEL_DIM)
        return lax.optimization_barrier(jnp.sum(picked * choice_weights[..., None], axis=1))
    expert_sum = lax.map(group_experts, (normed_mid.reshape(N_GRP, GROUP_TOKENS, MODEL_DIM), expert_ids.reshape(N_GRP, GROUP_TOKENS, TOP), route_weights.reshape(N_GRP, GROUP_TOKENS, TOP)))
    hidden_out = (mid_state.astype(jnp.float32) + expert_sum.reshape(TOKENS, MODEL_DIM)).astype(jnp.bfloat16)
    return (hidden_out, kv_cache)
```

```python
import functools

import jax
import jax.numpy as jnp
import numpy as np
from jax import lax
from jax.sharding import Mesh
from jax.sharding import PartitionSpec as P

AXES = ("y", "zl", "zh", "x", "c")
SIZES = (4, 8, 2, 4, 2)
ROW = ("x", "c")
PAGE = 16
CAP = 48


def permute(block, target):
    route = []
    for source in range(int(np.prod(SIZES))):
        place = dict(zip(AXES, (int(v) for v in np.unravel_index(source, SIZES))))
        goal = target(**place)
        if goal is not None:
            route.append((source, int(np.ravel_multi_index(goal, SIZES))))
    return lax.ppermute(block, AXES, route)


def swap_core(block):
    return permute(block, lambda y, zl, zh, x, c: (y, zl, zh, x, 1 - c))


def swap_half(block):
    return permute(block, lambda y, zl, zh, x, c: (y, zl, 1 - zh, x, c))


def swap_near(block):
    return permute(block, lambda y, zl, zh, x, c: (y, zl ^ 1, zh, x, c))


def next_group(block):
    def target(y, zl, zh, x, c):
        g = y * 8 + zl + 1
        return (g // 8, g % 8, zh, x, c) if zh == 0 and g < 32 else None

    return permute(block, target)


def ahead_x(block, step):
    return permute(block, lambda y, zl, zh, x, c: (y, zl, zh, (x - step) % 4, c))


def ahead_y(block, step):
    return permute(block, lambda y, zl, zh, x, c: ((y - step) % 4, zl, zh, x, c))


def from_all(block, ahead):
    one, three, two = [ahead(block, step) for step in (1, 3, 2)]
    return jnp.stack([block, one, two, three])


def in_order(relative, me):
    twice = jnp.concatenate([relative, relative], axis=0)
    return lax.dynamic_slice_in_dim(twice, (4 - me) % 4, 4, 0)


def rms_scale(row_data, gain_vec):
    values = row_data.astype(jnp.float32)
    inverse = lax.rsqrt(jnp.mean(values * values, axis=-1, keepdims=True) + 1e-05)
    return (values * inverse * gain_vec).astype(jnp.bfloat16)


def attend(queries, key_cat, value_cat, first_key, block_rows):
    rows = queries.shape[1]
    span = rows + block_rows
    outs = []
    for block in range(rows // block_rows):
        low = block * block_rows
        query = queries[:, low : low + block_rows]
        keys = key_cat[low : low + span]
        values = value_cat[low : low + span]
        position = low + jnp.arange(span, dtype=jnp.int32)
        own = rows + low + jnp.arange(block_rows, dtype=jnp.int32)
        allowed = (position[None, :] >= first_key[low : low + block_rows, None]) & (
            position[None, :] <= own[:, None]
        )
        scores = jnp.einsum("hqd,kd->hqk", query, keys, preferred_element_type=jnp.float32)
        scores = jnp.where(allowed[None], scores * 0.125, -1e30)
        exponent = jnp.exp(scores - jnp.max(scores, axis=-1, keepdims=True))
        weights = (exponent / jnp.sum(exponent, axis=-1, keepdims=True)).astype(jnp.bfloat16)
        result = jnp.einsum("hqk,kd->qhd", weights, values, preferred_element_type=jnp.float32)
        outs.append(result.astype(jnp.bfloat16).reshape(block_rows, -1))
    return jnp.concatenate(outs, axis=0)


def body(
    tokens,
    attn_gain,
    ffn_gain,
    w_query,
    key_value_weight,
    w_out,
    segment_ids,
    expert_ids,
    route_weights,
    w_gate,
    w_up,
    w_down,
    page_table,
):
    y, zl, zh, x, c = (lax.axis_index(name) for name in AXES)
    width = tokens.shape[1]
    tok = tokens.shape[0]
    rows = 8 * tok

    own_pack = jnp.concatenate([w_query.T, key_value_weight.T, w_out], axis=0)
    part = own_pack.shape[0] // 4
    far_part = swap_half(lax.dynamic_slice_in_dim(own_pack, y * part, part, 0))
    far_pack = in_order(from_all(far_part, ahead_y), y).reshape(-1, width)
    own_cols, far_cols = own_pack[:128], far_pack[:128]
    other_own = swap_core(own_cols)
    other_far = swap_core(far_cols)

    normed_in = rms_scale(tokens, attn_gain)
    near = from_all(normed_in, ahead_x).reshape(4 * tok, width)

    def project(cols):
        return lax.dot_general(
            near, cols, (((1,), (1,)), ((), ())), preferred_element_type=jnp.float32
        ).astype(jnp.bfloat16)

    keep = jnp.concatenate([project(own_cols), project(far_cols)], axis=1)
    give = jnp.concatenate([project(other_own), project(other_far)], axis=1)
    got = swap_core(give)
    both = jnp.where(c == 0, jnp.stack([keep, got]), jnp.stack([got, keep]))
    both = both.reshape(2, 4, tok, 256).transpose(1, 0, 2, 3)
    projected = in_order(both, x).reshape(rows, 256)
    queries = jnp.stack([projected[:, 0:64], projected[:, 128:192]])
    own_kv, far_kv = projected[:, 64:128], projected[:, 192:256]
    key_rows = jnp.where(zh == 0, own_kv, far_kv)
    value_rows = jnp.where(zh == 0, far_kv, own_kv)
    key_value = jnp.concatenate([key_rows, value_rows], axis=1)

    partner = swap_half(key_value)
    shifted = next_group(partner)
    before = jnp.where(zh == 0, shifted, partner)

    seg_near = from_all(segment_ids, ahead_x)
    seg_got = swap_core(seg_near)
    seg = jnp.where(c == 0, jnp.stack([seg_near, seg_got]), jnp.stack([seg_got, seg_near]))
    seg = in_order(seg.transpose(1, 0, 2), x).reshape(rows)
    base = ((y * 8 + zl) * 2 + zh) * rows
    first_key = seg - base + rows

    key_cat = jnp.concatenate([before[:, :64], key_rows], axis=0)
    value_cat = jnp.concatenate([before[:, 64:], value_rows], axis=0)
    attended = attend(queries, key_cat, value_cat, first_key, 512)

    group_kv = jnp.where(
        zh == 0, jnp.stack([key_value, partner]), jnp.stack([partner, key_value])
    )
    page_order = page_table[0]
    page_ids = zh * 64 + jnp.arange(64, dtype=jnp.int32)
    block_ids = jnp.arange(128, dtype=jnp.int32)
    source_block = jnp.sum(
        jnp.where(page_order[None, :] == page_ids[:, None], block_ids[None, :], 0), axis=1
    )
    pages = group_kv.reshape(128, PAGE, 128)[source_block]

    joined = jnp.concatenate(
        [attended.reshape(8, tok, 128), pages.reshape(8, tok, 128)], axis=1
    )
    joined = lax.all_to_all(joined, ROW, split_axis=0, concat_axis=0, tiled=True)
    token_heads = joined[:, :tok].transpose(1, 0, 2).reshape(tok, 1024)
    kv_cache = joined[:, tok:].reshape(8, 8, PAGE, 2, 64).transpose(1, 2, 3, 0, 4)
    kv_cache = kv_cache.reshape(8, PAGE, 1024)

    out_rows = jnp.concatenate([own_pack[128:], far_pack[128:]], axis=0)
    out_all = lax.all_gather(out_rows, ROW, axis=0, tiled=True)
    out_sum = jnp.dot(token_heads, out_all, preferred_element_type=jnp.float32)
    mid_state = (tokens.astype(jnp.float32) + out_sum).astype(jnp.bfloat16)
    normed_mid = rms_scale(mid_state, ffn_gain)

    gate_up = jnp.concatenate([w_gate, w_up], axis=1)
    piece = y * 2 + zl % 2

    def far_weight(own):
        step = own.shape[0] // 8
        eighth = swap_half(lax.dynamic_slice_in_dim(own, piece * step, step, 0))
        beside = swap_near(eighth)
        pair = jnp.where(
            zl % 2 == 0,
            jnp.concatenate([eighth, beside], axis=0),
            jnp.concatenate([beside, eighth], axis=0),
        )
        return lax.all_gather(pair, "y", axis=0, tiled=True)

    def whole(own):
        far = far_weight(own)
        mine = c == zh
        kept = jnp.where(mine, own, far)
        return kept, swap_core(jnp.where(mine, far, own))

    gate_up_a, gate_up_b = whole(gate_up)
    down_a, down_b = whole(w_down)

    flat = expert_ids.reshape(-1)
    onehot = (flat[:, None] == jnp.arange(8, dtype=jnp.int32)[None, :]).astype(jnp.int32)
    earlier = jnp.cumsum(onehot, axis=0) - onehot
    slot = jnp.sum(earlier * onehot, axis=-1)
    holder = (flat % 4) * 2 + flat // 4
    target_slot = (holder * CAP + slot).reshape(tok, 2)
    slots = jnp.arange(8 * CAP, dtype=jnp.int32)
    pick = [
        (target_slot[:, k : k + 1] == slots[None, :]).astype(jnp.bfloat16) for k in range(2)
    ]
    send = lax.dot_general(
        pick[0] + pick[1],
        normed_mid,
        (((0,), (0,)), ((), ())),
        preferred_element_type=jnp.float32,
    ).astype(jnp.bfloat16)
    arrived = lax.all_to_all(
        send.reshape(8, CAP, width), ROW, split_axis=0, concat_axis=0, tiled=True
    ).reshape(8 * CAP, width)

    def half(gate_up_half, down_half):
        both_act = jnp.dot(arrived, gate_up_half, preferred_element_type=jnp.float32)
        gate_act, up_act = both_act[:, :256], both_act[:, 256:]
        activated = (jax.nn.silu(gate_act) * up_act).astype(jnp.bfloat16)
        return jnp.dot(activated, down_half, preferred_element_type=jnp.float32)

    expert_out = (half(gate_up_a, down_a) + half(gate_up_b, down_b)).astype(jnp.bfloat16)
    returned = lax.all_to_all(
        expert_out.reshape(8, CAP, width), ROW, split_axis=0, concat_axis=0, tiled=True
    ).reshape(8 * CAP, width)
    total = mid_state.astype(jnp.float32)
    for k in range(2):
        chosen = jnp.dot(pick[k], returned, preferred_element_type=jnp.float32)
        total = total + chosen * route_weights[:, k : k + 1]
    return (total.astype(jnp.bfloat16), kv_cache)


def solution(mesh):
    fine = Mesh(mesh.devices.reshape(SIZES), AXES)
    grp, tp = ("y", "zl"), ("zh", "x", "c")
    in_specs = (
        P(AXES, None),
        P(),
        P(),
        P(None, tp),
        P(None, tp),
        P(tp, None),
        P(AXES),
        P(AXES, None),
        P(AXES, None),
        P(None, tp),
        P(None, tp),
        P(tp, None),
        P(grp, None),
    )
    out_specs = (P(AXES, None), P(AXES, None, None))
    return jax.shard_map(body, mesh=fine, in_specs=in_specs, out_specs=out_specs, check_vma=False)
```

```python
import functools

import jax
import jax.numpy as jnp
import numpy as np
from jax import lax
from jax.experimental import pallas as pl
from jax.experimental.pallas import tpu as pltpu
from jax.sharding import Mesh
from jax.sharding import PartitionSpec as P

AXES = ("y", "zl", "zh", "x", "c")
SIZES = (4, 8, 2, 4, 2)
ROW = ("x", "c")
PAGE = 16
CAP = 48
TOK = 128
WIDTH = 1536
ROWS = 8 * TOK
BF16 = jnp.bfloat16
F32 = jnp.float32
I32 = jnp.int32
VMEM = pl.BlockSpec(memory_space=pltpu.VMEM)
SMEM = pl.BlockSpec(memory_space=pltpu.SMEM)
MIB = 1 << 20


def permute(block, target):
    route = []
    for source in range(int(np.prod(SIZES))):
        place = dict(zip(AXES, (int(v) for v in np.unravel_index(source, SIZES))))
        goal = target(**place)
        if goal is not None:
            route.append((source, int(np.ravel_multi_index(goal, SIZES))))
    return lax.ppermute(block, AXES, route)


def swap_core(block):
    return permute(block, lambda y, zl, zh, x, c: (y, zl, zh, x, 1 - c))


def swap_half(block):
    return permute(block, lambda y, zl, zh, x, c: (y, zl, 1 - zh, x, c))


def swap_near(block):
    return permute(block, lambda y, zl, zh, x, c: (y, zl ^ 1, zh, x, c))


def next_group(block):
    def target(y, zl, zh, x, c):
        g = y * 8 + zl + 1
        return (g // 8, g % 8, zh, x, c) if zh == 0 and g < 32 else None

    return permute(block, target)


def ahead_x(block, step):
    return permute(block, lambda y, zl, zh, x, c: (y, zl, zh, (x - step) % 4, c))


def ahead_y(block, step):
    return permute(block, lambda y, zl, zh, x, c: ((y - step) % 4, zl, zh, x, c))


def after(value, *earlier):
    return lax.optimization_barrier((value,) + earlier)[0]


def call(kernel, outs, in_specs, scratch=(), flops=0, nbytes=0, limit=48):
    outs = [jax.ShapeDtypeStruct(shape, kind) for shape, kind in outs]
    return pl.pallas_call(
        kernel,
        out_shape=outs,
        in_specs=in_specs,
        out_specs=[VMEM] * len(outs),
        scratch_shapes=list(scratch),
        compiler_params=pltpu.CompilerParams(vmem_limit_bytes=limit * MIB),
        cost_estimate=pl.CostEstimate(flops=flops, bytes_accessed=nbytes, transcendentals=0),
    )


def dot_nt(left, right):
    return lax.dot_general(left, right, (((1,), (1,)), ((), ())), preferred_element_type=F32)


def dot_tn(left, right):
    return lax.dot_general(left, right, (((0,), (0,)), ((), ())), preferred_element_type=F32)


def column(lane_row):
    return jnp.transpose(jnp.broadcast_to(lane_row, (TOK, TOK)))


def rms(values, gain):
    inverse = lax.rsqrt(jnp.mean(values * values, axis=-1, keepdims=True) + 1e-05)
    return (values * inverse * gain).astype(BF16)


def norm_kernel(meta, tokens, gain, seg, out):
    out[:TOK] = rms(tokens[...].astype(F32), gain[...])
    own = meta[5] * TOK + lax.broadcasted_iota(I32, (1, TOK), 1)
    back = own - seg[...]
    row = lax.broadcasted_iota(I32, (16, TOK), 0)
    pieces = jnp.where(row == 0, back >> 5, jnp.where(row == 1, back & 31, 0))
    out[TOK:, :TOK] = pieces.astype(F32).astype(BF16)
    out[TOK:, TOK:] = jnp.zeros((16, WIDTH - TOK), BF16)


def project_kernel(meta, b0, b1, b2, b3, s0, s1, s2, s3, wq, wkv, wo, f0, f1, f2, f3,
                   q_out, kv_out, start_out, wo_out, far, cols):
    y, zh, x, c = meta[0], meta[2], meta[3], meta[4]
    for k, part in enumerate((f0, f1, f2, f3)):
        low = pl.multiple_of(lax.rem(y + k, 4) * 48, 16)
        far[pl.ds(low, 48), :] = part[...]
    cols[0:64] = wq[...]
    cols[64:128] = far[0:64]
    key_low = pl.multiple_of(128 + zh * 64, 64)
    value_low = pl.multiple_of(192 - zh * 64, 64)
    cols[pl.ds(key_low, 64), :] = wkv[...]
    cols[pl.ds(value_low, 64), :] = far[64:128]
    wo_out[0:64] = wo[...]
    wo_out[64:128] = far[128:192]
    for k in range(4):
        place = lax.rem(x + k, 4) * 2
        for block, core in (((b0, b1, b2, b3)[k], c), ((s0, s1, s2, s3)[k], 1 - c)):
            low = pl.multiple_of((place + core) * TOK, TOK)
            result = dot_nt(block[:TOK], cols[...]).astype(BF16)
            q_out[pl.ds(low, TOK), :] = result[:, :128]
            kv_out[pl.ds(low, TOK), :] = result[:, 128:]
            pieces = block[TOK:, :TOK].astype(F32)
            back = column(pieces[0:1] * 32.0 + pieces[1:2])
            own = (low + lax.broadcasted_iota(I32, (TOK, TOK), 0)).astype(F32)
            start_out[pl.ds(low, TOK), :] = own - back


def split_kv(kv):
    wide = kv[...].astype(F32)
    turned = pltpu.roll(wide, 64, 1)
    low = lax.broadcasted_iota(I32, wide.shape, 1) < 64
    return (
        jnp.where(low, wide, turned).astype(BF16),
        jnp.where(low, turned, wide).astype(BF16),
    )


STEP = 256


def own_kernel(q, kv, start, ids, sum_out, max_out, den_out, slots_out, keys, values):
    keys[...], values[...] = split_kv(kv)
    low_lane = lax.broadcasted_iota(I32, (STEP, 128), 1) < 64
    for block in range(ROWS // STEP):
        low = block * STEP
        span = low + STEP
        query = q[low:span]
        position = lax.broadcasted_iota(I32, (STEP, span), 1).astype(F32)
        own = (low + lax.broadcasted_iota(I32, (STEP, span), 0)).astype(F32)
        allowed = (position <= own) & (position >= start[low:span, 0:1])
        parts = []
        for head in range(2):
            kept = jnp.where(low_lane if head == 0 else ~low_lane, query, jnp.zeros_like(query))
            scores = jnp.where(allowed, dot_nt(kept, keys[:span]) * 0.125, -1e30)
            top = jnp.max(scores, axis=-1, keepdims=True)
            weights = jnp.exp(scores - top)
            den = jnp.sum(weights, axis=-1, keepdims=True)
            part = jnp.dot(weights.astype(BF16), values[:span], preferred_element_type=F32)
            parts.append((part, top, den))
        for out, one, two in zip((sum_out, max_out, den_out), *parts):
            out[low:span] = jnp.where(low_lane, one, two)
    choice = [ids[k : k + 1].astype(F32) for k in range(2)]
    down = [column(v) for v in choice]
    earlier = lax.broadcasted_iota(I32, (TOK, TOK), 0) < lax.broadcasted_iota(I32, (TOK, TOK), 1)
    result = []
    for k in range(2):
        same = sum((down[j] == choice[k]).astype(F32) for j in range(2))
        rank = jnp.sum(jnp.where(earlier, same, 0.0), axis=0, keepdims=True).astype(I32)
        expert = ids[k : k + 1]
        result.append(((expert & 3) * 2 + (expert >> 2)) * CAP + rank)
    row = lax.broadcasted_iota(I32, (8, TOK), 0)
    slots_out[...] = jnp.where(row == 0, result[0], result[1])


def before_kernel(meta, table, q, kv, partner, shifted, start, sums, maxes, dens,
                  out, keys, values, group):
    zh = meta[2]

    @pl.when(zh == 0)
    def _():
        keys[...], values[...] = split_kv(shifted)

    @pl.when(zh != 0)
    def _():
        keys[...], values[...] = split_kv(partner)

    low_lane = lax.broadcasted_iota(I32, (STEP, 128), 1) < 64
    for block in range(ROWS // STEP):
        low = block * STEP
        high = low + STEP
        span = ROWS - low
        query = q[low:high]
        position = (low - ROWS + lax.broadcasted_iota(I32, (STEP, span), 1)).astype(F32)
        allowed = position >= start[low:high, 0:1]
        parts = []
        for head in range(2):
            kept = jnp.where(low_lane if head == 0 else ~low_lane, query, jnp.zeros_like(query))
            scores = jnp.where(allowed, dot_nt(kept, keys[low:]) * 0.125, -1e30)
            first = maxes[low:high, head * 64 : head * 64 + 1]
            top = jnp.maximum(first, jnp.max(scores, axis=-1, keepdims=True))
            weights = jnp.exp(scores - top)
            scale = jnp.exp(first - top)
            den = jnp.sum(weights, axis=-1, keepdims=True)
            part = jnp.dot(weights.astype(BF16), values[low:], preferred_element_type=F32)
            parts.append((part, scale, den))
        part, scale, den = (jnp.where(low_lane, one, two) for one, two in zip(*parts))
        total = sums[low:high] * scale + part
        result = (total / (dens[low:high] * scale + den)).astype(BF16)
        for j in range(STEP // TOK):
            out[low // TOK + j, :TOK, :] = result[j * TOK : (j + 1) * TOK]
    group[pl.ds(pl.multiple_of(zh * ROWS, ROWS), ROWS), :] = kv[...]
    group[pl.ds(pl.multiple_of((1 - zh) * ROWS, ROWS), ROWS), :] = partner[...]

    def place(block, carry):
        page = table[0, block] - zh * 64

        @pl.when((page >= 0) & (page < 64))
        def _():
            low = pl.multiple_of(TOK + lax.rem(page, 8) * PAGE, PAGE)
            out[page // 8, pl.ds(low, PAGE), :] = group[
                pl.ds(pl.multiple_of(block * PAGE, PAGE), PAGE), :
            ]

        return carry

    lax.fori_loop(0, 128, place, 0)


def cache_kernel(joined, out):
    low = lax.broadcasted_iota(I32, (TOK, 128), 1) < 64
    for pair in range(4):
        one = joined[2 * pair, TOK:, :].astype(F32)
        two = joined[2 * pair + 1, TOK:, :].astype(F32)
        lanes = slice(pair * 128, pair * 128 + 128)
        out[:, lanes] = jnp.where(low, one, pltpu.roll(two, 64, 1)).astype(BF16)
        lanes = slice(512 + pair * 128, 640 + pair * 128)
        out[:, lanes] = jnp.where(low, pltpu.roll(one, 64, 1), two).astype(BF16)


def choose(slots, k):
    place = lax.broadcasted_iota(I32, (8 * CAP, TOK), 0)
    return place == slots[k : k + 1]


def mid_kernel(joined, wo_all, tokens, gain, slots, mid_out, send_out):
    heads = jnp.concatenate([joined[j, :TOK, :] for j in range(8)], axis=1)
    total = jnp.dot(heads, wo_all[...], preferred_element_type=F32)
    mid = (tokens[...].astype(F32) + total).astype(BF16)
    mid_out[...] = mid
    normed = rms(mid.astype(F32), gain[...])
    pick = (choose(slots, 0) | choose(slots, 1)).astype(F32).astype(BF16)
    send_out[...] = jnp.dot(pick, normed, preferred_element_type=F32).astype(BF16)


def expert_kernel(arrived, kept, given, out):
    acts = []
    for half in (kept, given):
        both = jnp.dot(arrived[...], half[:WIDTH], preferred_element_type=F32)
        gate, up = both[:, :256], both[:, 256:]
        acts.append((gate / (1.0 + jnp.exp(-gate)) * up).astype(BF16))
    for chunk in range(3):
        rows = slice(WIDTH + chunk * 256, WIDTH + chunk * 256 + 256)
        total = jnp.dot(acts[0], kept[rows], preferred_element_type=F32)
        total += jnp.dot(acts[1], given[rows], preferred_element_type=F32)
        out[:, chunk * 512 : chunk * 512 + 512] = total.astype(BF16)


def combine_kernel(returned, mid, slots, weights, out):
    total = mid[...].astype(F32)
    for k in range(2):
        pick = choose(slots, k).astype(F32).astype(BF16)
        chosen = dot_tn(pick, returned[...])
        total += chosen * column(weights[k : k + 1])[:, 0:1]
    out[...] = total.astype(BF16)


def body(
    tokens,
    attn_gain,
    ffn_gain,
    w_query,
    key_value_weight,
    w_out,
    segment_ids,
    expert_ids,
    route_weights,
    w_gate,
    w_up,
    w_down,
    page_table,
):
    y, zl, zh, x, c = (lax.axis_index(name) for name in AXES)
    place = (((y * 8 + zl) * 2 + zh) * 4 + x) * 2 + c
    meta = jnp.stack([y, zl, zh, x, c, place]).astype(I32)
    wq, wkv = w_query.T, key_value_weight.T

    own_pack = jnp.concatenate([wq, wkv, w_out], axis=0)
    far = [swap_half(lax.dynamic_slice_in_dim(own_pack, y * 48, 48, 0))]
    (block,) = call(
        norm_kernel, [((TOK + 16, WIDTH), BF16)], [SMEM, VMEM, VMEM, VMEM], nbytes=800000
    )(meta, tokens, attn_gain[None, :], segment_ids[None, :])
    near = [block] + [ahead_x(block, step) for step in (1, 3, 2)]
    far += [ahead_y(far[0], step) for step in (1, 3, 2)]
    across = [swap_core(part) for part in near]
    order = (0, 1, 3, 2)
    q, kv, start, out_rows = call(
        project_kernel,
        [((ROWS, 128), BF16), ((ROWS, 128), BF16), ((ROWS, 128), F32), ((128, WIDTH), BF16)],
        [SMEM] + [VMEM] * 15,
        scratch=[pltpu.VMEM((192, WIDTH), BF16), pltpu.VMEM((256, WIDTH), BF16)],
        flops=2 * ROWS * WIDTH * 256,
        nbytes=5000000,
    )(
        meta,
        *[near[i] for i in order],
        *[across[i] for i in order],
        wq,
        wkv,
        w_out,
        *[far[i] for i in order],
    )
    out_all = lax.all_gather(out_rows, ROW, axis=0, tiled=True)

    partner = swap_half(kv)
    shifted = next_group(partner)
    sums, maxes, dens, slots = call(
        own_kernel,
        [((ROWS, 128), F32)] * 3 + [((8, TOK), I32)],
        [VMEM] * 4,
        scratch=[pltpu.VMEM((ROWS, 128), BF16)] * 2,
        flops=1000000000,
        nbytes=3000000,
    )(q, kv, start, expert_ids.T)
    (joined,) = call(
        before_kernel,
        [((8, 2 * TOK, 128), BF16)],
        [SMEM, SMEM] + [VMEM] * 8,
        scratch=[pltpu.VMEM((ROWS, 128), BF16)] * 2 + [pltpu.VMEM((2 * ROWS, 128), BF16)],
        flops=1000000000,
        nbytes=3000000,
    )(meta, page_table, q, kv, partner, shifted, start, sums, maxes, dens)
    joined = lax.all_to_all(joined, ROW, split_axis=0, concat_axis=0, tiled=True)

    mid, send = call(
        mid_kernel,
        [((TOK, WIDTH), BF16), ((8 * CAP, WIDTH), BF16)],
        [VMEM] * 5,
        flops=600000000,
        nbytes=5000000,
    )(joined, out_all, tokens, ffn_gain[None, :], slots)
    arrived = lax.all_to_all(
        send.reshape(8, CAP, WIDTH), ROW, split_axis=0, concat_axis=0, tiled=True
    ).reshape(8 * CAP, WIDTH)
    (cache,) = call(cache_kernel, [((TOK, 1024), BF16)], [VMEM], nbytes=800000)(joined)

    w_gate, w_up, w_down = (after(w, block) for w in (w_gate, w_up, w_down))
    own = jnp.concatenate(
        [jnp.concatenate([w_gate, w_up], axis=1)] + [w_down[:, i : i + 512] for i in (0, 512, 1024)],
        axis=0,
    )
    eighth = lax.dynamic_slice_in_dim(own, (y * 2 + zl % 2) * 288, 288, 0)
    eighth = swap_half(after(eighth, far[0]))
    beside = swap_near(eighth)
    pair = jnp.where(
        zl % 2 == 0,
        jnp.concatenate([eighth, beside], axis=0),
        jnp.concatenate([beside, eighth], axis=0),
    )
    other = lax.all_gather(pair, "y", axis=0, tiled=True)
    mine = c == zh
    kept = jnp.where(mine, own, other)
    given = swap_core(jnp.where(mine, other, own))
    (expert_out,) = call(
        expert_kernel,
        [((8 * CAP, WIDTH), BF16)],
        [VMEM] * 3,
        flops=1800000000,
        nbytes=7000000,
    )(arrived, kept, given)
    returned = lax.all_to_all(
        expert_out.reshape(8, CAP, WIDTH), ROW, split_axis=0, concat_axis=0, tiled=True
    ).reshape(8 * CAP, WIDTH)
    (hidden,) = call(
        combine_kernel, [((TOK, WIDTH), BF16)], [VMEM] * 4, flops=300000000, nbytes=2000000
    )(returned, mid, slots, route_weights.T)
    return (hidden, cache.reshape(8, PAGE, 1024))


def solution(mesh):
    fine = Mesh(mesh.devices.reshape(SIZES), AXES)
    grp, tp = ("y", "zl"), ("zh", "x", "c")
    in_specs = (
        P(AXES, None),
        P(),
        P(),
        P(None, tp),
        P(None, tp),
        P(tp, None),
        P(AXES),
        P(AXES, None),
        P(AXES, None),
        P(None, tp),
        P(None, tp),
        P(tp, None),
        P(grp, None),
    )
    out_specs = (P(AXES, None), P(AXES, None, None))
    return jax.shard_map(body, mesh=fine, in_specs=in_specs, out_specs=out_specs, check_vma=False)
```

```python
import functools

import jax
import jax.numpy as jnp
import numpy as np
from jax import lax
from jax.experimental import pallas as pl
from jax.experimental.pallas import tpu as pltpu
from jax.sharding import Mesh
from jax.sharding import PartitionSpec as P

AXES = ("y", "zq", "zp", "zh", "x", "c")
SIZES = (4, 4, 2, 2, 4, 2)
FLAT = (4, 8, 2, 4, 2)
ROW = ("x", "c")
PAGE = 16
CAP = 48
TOK = 128
WIDTH = 1536
ROWS = 8 * TOK
BF16 = jnp.bfloat16
F32 = jnp.float32
I32 = jnp.int32
VMEM = pl.BlockSpec(memory_space=pltpu.VMEM)
ANY = pl.BlockSpec(memory_space=pl.ANY)
SMEM = pl.BlockSpec(memory_space=pltpu.SMEM)
MIB = 1 << 20


def permute(block, target):
    route = []
    for source in range(int(np.prod(FLAT))):
        goal = target(*(int(v) for v in np.unravel_index(source, FLAT)))
        if goal is not None:
            route.append((source, int(np.ravel_multi_index(goal, FLAT))))
    return lax.ppermute(block, AXES, route)


def swap_core(block):
    return permute(block, lambda y, zl, zh, x, c: (y, zl, zh, x, 1 - c))


def swap_half(block):
    return permute(block, lambda y, zl, zh, x, c: (y, zl, 1 - zh, x, c))


def next_group(block):
    def target(y, zl, zh, x, c):
        if zl < 7:
            return (y, zl + 1, 0, x, c) if zh == 0 else None
        return (y + 1, 0, 0, x, c) if zh == 1 and y < 3 else None

    return permute(block, target)


def give_half(block, near):
    def target(y, zl, zh, x, c):
        return (y, zl, zh, x, 1 - c) if (c == zh) != near else None

    return permute(block, target)


def gather(block, axis):
    wide = jnp.broadcast_to(block[None], (lax.axis_size(axis),) + block.shape)
    return lax.all_to_all(wide, axis, split_axis=0, concat_axis=0, tiled=True)


def after(value, *earlier):
    return lax.optimization_barrier((value,) + earlier)[0]


def call(kernel, outs, in_specs, scratch=(), flops=0, nbytes=0, limit=48):
    outs = [jax.ShapeDtypeStruct(shape, kind) for shape, kind in outs]
    return pl.pallas_call(
        kernel,
        out_shape=outs,
        in_specs=in_specs,
        out_specs=[VMEM] * len(outs),
        scratch_shapes=list(scratch),
        compiler_params=pltpu.CompilerParams(vmem_limit_bytes=limit * MIB),
        cost_estimate=pl.CostEstimate(flops=flops, bytes_accessed=nbytes, transcendentals=0),
    )


def dot_nt(left, right):
    return lax.dot_general(left, right, (((1,), (1,)), ((), ())), preferred_element_type=F32)


def dot_tn(left, right):
    return lax.dot_general(left, right, (((0,), (0,)), ((), ())), preferred_element_type=F32)


def column(lane_row):
    return jnp.transpose(jnp.broadcast_to(lane_row, (TOK, TOK)))


def rms(values, gain):
    inverse = lax.rsqrt(jnp.mean(values * values, axis=-1, keepdims=True) + 1e-05)
    return (values * inverse * gain).astype(BF16)


def pack_kernel(meta, tokens, seg, ids, out):
    own = meta[5] * TOK + lax.broadcasted_iota(I32, (1, TOK), 1)
    back = own - seg[...]
    row = lax.broadcasted_iota(I32, (16, TOK), 0)
    pieces = jnp.where(row == 0, back >> 5, jnp.where(row == 1, back & 31, 0))
    pieces = jnp.where(row == 2, ids[0:1], jnp.where(row == 3, ids[1:2], pieces))
    pieces = pieces.astype(F32).astype(BF16)
    for copy in range(4):
        out[copy, :TOK] = tokens[...]
        out[copy, TOK:, :TOK] = pieces
        out[copy, TOK:, TOK:] = jnp.zeros((16, WIDTH - TOK), BF16)


def eighth_kernel(meta, gate, up, down, out, sems):
    piece = meta[0] * 2 + lax.rem(meta[1], 2)
    wide = pl.ds(pl.multiple_of(piece * 192, 64), 192)
    deep = pl.ds(pl.multiple_of(piece * 32, 32), 32)
    copies = [
        pltpu.make_async_copy(gate.at[wide], out.at[:192, :256], sems.at[0]),
        pltpu.make_async_copy(up.at[wide], out.at[:192, 256:], sems.at[1]),
    ]
    for i in range(3):
        copies.append(
            pltpu.make_async_copy(
                down.at[deep, i * 512 : i * 512 + 512],
                out.at[192 + 32 * i : 224 + 32 * i],
                sems.at[2 + i],
            )
        )
    for copy in copies:
        copy.start()
    for copy in copies:
        copy.wait()


def order_kernel(gate, up, down, out):
    for e in range(8):
        low = e * 288
        out[low : low + 192, :256] = gate[e * 192 : e * 192 + 192]
        out[low : low + 192, 256:] = up[e * 192 : e * 192 + 192]
        for i in range(3):
            out[low + 192 + 32 * i : low + 224 + 32 * i] = down[
                e * 32 : e * 32 + 32, i * 512 : i * 512 + 512
            ]


def project_kernel(meta, near, across, wq, wkv, far, gain, q_out, kv_out, start_out, cols):
    zh, c = meta[2], meta[4]
    cols[0:64] = wq[...]
    cols[64:128] = far[0:64]
    cols[pl.ds(pl.multiple_of(128 + zh * 64, 64), 64), :] = wkv[...]
    cols[pl.ds(pl.multiple_of(192 - zh * 64, 64), 64), :] = far[64:128]
    for k in range(4):
        for block, core in ((near, c), (across, 1 - c)):
            low = pl.multiple_of((2 * k + core) * TOK, TOK)
            normed = rms(block[k, :TOK].astype(F32), gain[...])
            result = dot_nt(normed, cols[...]).astype(BF16)
            q_out[pl.ds(low, TOK), :] = result[:, :128]
            kv_out[pl.ds(low, TOK), :] = result[:, 128:]
            pieces = block[k, TOK:, :TOK].astype(F32)
            back = column(pieces[0:1] * 32.0 + pieces[1:2])
            own = (low + lax.broadcasted_iota(I32, (TOK, TOK), 0)).astype(F32)
            start_out[pl.ds(low, TOK), :] = own - back


def route_kernel(meta, near, across, pick_out, other_out, rows_out):
    x, c = meta[3], meta[4]
    before = lax.broadcasted_iota(I32, (TOK, TOK), 0) < lax.broadcasted_iota(I32, (TOK, TOK), 1)
    before = before.astype(F32).astype(BF16)
    row = lax.broadcasted_iota(I32, (CAP, TOK), 0).astype(F32)
    for expert, out in ((x + 4 * c, pick_out), (x + 4 * (1 - c), other_out)):
        number = expert.astype(F32)
        for k in range(4):
            for block, core in ((near, c), (across, 1 - c)):
                low = pl.multiple_of((2 * k + core) * CAP, 16)
                pieces = block[k, TOK:, :TOK].astype(F32)
                named = (pieces == number).astype(F32)
                named = named[2:3] + named[3:4]
                rank = jnp.dot(
                    jnp.broadcast_to(named, (8, TOK)).astype(BF16),
                    before,
                    preferred_element_type=F32,
                )[0:1]
                pick = jnp.where((row == rank) & (named > 0.0), 1.0, 0.0).astype(BF16)
                out[pl.ds(low, CAP), :] = pick
                if out is pick_out:
                    chosen = jnp.dot(pick, block[k, :TOK], preferred_element_type=F32)
                    rows_out[pl.ds(low, CAP), :] = chosen.astype(BF16)


def split_kv(kv):
    wide = kv[...].astype(F32)
    turned = pltpu.roll(wide, 64, 1)
    low = lax.broadcasted_iota(I32, wide.shape, 1) < 64
    return (
        jnp.where(low, wide, turned).astype(BF16),
        jnp.where(low, turned, wide).astype(BF16),
    )


STEP = 256


def own_kernel(q, kv, start, ids, sum_out, max_out, den_out, slots_out, keys, values):
    keys[...], values[...] = split_kv(kv)
    low_lane = lax.broadcasted_iota(I32, (STEP, 128), 1) < 64
    for block in range(ROWS // STEP):
        low = block * STEP
        span = low + STEP
        query = q[low:span]
        position = lax.broadcasted_iota(I32, (STEP, span), 1).astype(F32)
        own = (low + lax.broadcasted_iota(I32, (STEP, span), 0)).astype(F32)
        allowed = (position <= own) & (position >= start[low:span, 0:1])
        parts = []
        for head in range(2):
            kept = jnp.where(low_lane if head == 0 else ~low_lane, query, jnp.zeros_like(query))
            scores = jnp.where(allowed, dot_nt(kept, keys[:span]) * 0.125, -1e30)
            top = jnp.max(scores, axis=-1, keepdims=True)
            weights = jnp.exp(scores - top)
            den = jnp.sum(weights, axis=-1, keepdims=True)
            part = jnp.dot(weights.astype(BF16), values[:span], preferred_element_type=F32)
            parts.append((part, top, den))
        for out, one, two in zip((sum_out, max_out, den_out), *parts):
            out[low:span] = jnp.where(low_lane, one, two)
    choice = [ids[k : k + 1].astype(F32) for k in range(2)]
    down = [column(v) for v in choice]
    earlier = lax.broadcasted_iota(I32, (TOK, TOK), 0) < lax.broadcasted_iota(I32, (TOK, TOK), 1)
    result = []
    for k in range(2):
        same = sum((down[j] == choice[k]).astype(F32) for j in range(2))
        rank = jnp.sum(jnp.where(earlier, same, 0.0), axis=0, keepdims=True).astype(I32)
        expert = ids[k : k + 1]
        result.append(((expert & 3) * 2 + (expert >> 2)) * CAP + rank)
    row = lax.broadcasted_iota(I32, (8, TOK), 0)
    slots_out[...] = jnp.where(row == 0, result[0], result[1])


def before_kernel(q, kv, start, sums, maxes, dens, out, keys, values):
    keys[...], values[...] = split_kv(kv)
    low_lane = lax.broadcasted_iota(I32, (STEP, 128), 1) < 64
    for block in range(ROWS // STEP):
        low = block * STEP
        high = low + STEP
        span = ROWS - low
        query = q[low:high]
        position = (low - ROWS + lax.broadcasted_iota(I32, (STEP, span), 1)).astype(F32)
        allowed = position >= start[low:high, 0:1]
        parts = []
        for head in range(2):
            kept = jnp.where(low_lane if head == 0 else ~low_lane, query, jnp.zeros_like(query))
            scores = jnp.where(allowed, dot_nt(kept, keys[low:]) * 0.125, -1e30)
            first = maxes[low:high, head * 64 : head * 64 + 1]
            top = jnp.maximum(first, jnp.max(scores, axis=-1, keepdims=True))
            weights = jnp.exp(scores - top)
            scale = jnp.exp(first - top)
            den = jnp.sum(weights, axis=-1, keepdims=True)
            part = jnp.dot(weights.astype(BF16), values[low:], preferred_element_type=F32)
            parts.append((part, scale, den))
        part, scale, den = (jnp.where(low_lane, one, two) for one, two in zip(*parts))
        total = sums[low:high] * scale + part
        result = (total / (dens[low:high] * scale + den)).astype(BF16)
        for copy in range(4):
            out[copy, low:high, :] = result


def page_kernel(meta, table, kv, partner, out, group):
    zh = meta[2]
    group[pl.ds(pl.multiple_of(zh * ROWS, ROWS), ROWS), :] = kv[...]
    group[pl.ds(pl.multiple_of((1 - zh) * ROWS, ROWS), ROWS), :] = partner[...]

    def place(block, carry):
        page = table[0, block] - zh * 64

        @pl.when((page >= 0) & (page < 64))
        def _():
            out[pl.ds(pl.multiple_of(page * PAGE, PAGE), PAGE), :] = group[
                pl.ds(pl.multiple_of(block * PAGE, PAGE), PAGE), :
            ]

        return carry

    lax.fori_loop(0, 128, place, 0)


def cache_kernel(pages, out):
    low = lax.broadcasted_iota(I32, (TOK, 128), 1) < 64
    for pair in range(4):
        one = pages[2 * pair].astype(F32)
        two = pages[2 * pair + 1].astype(F32)
        lanes = slice(pair * 128, pair * 128 + 128)
        out[:, lanes] = jnp.where(low, one, pltpu.roll(two, 64, 1)).astype(BF16)
        lanes = slice(512 + pair * 128, 640 + pair * 128)
        out[:, lanes] = jnp.where(low, pltpu.roll(one, 64, 1), two).astype(BF16)


def choose(slots, k):
    place = lax.broadcasted_iota(I32, (8 * CAP, TOK), 0)
    return place == slots[k : k + 1]


def split_kernel(meta, heads, pick, other, keep_out, give_out):
    x, c = meta[3], meta[4]
    for d in range(8):
        rows = jnp.concatenate([heads[k, d * TOK : d * TOK + TOK] for k in range(4)], axis=1)
        low = slice(d * CAP, d * CAP + CAP)
        keep_out[low] = jnp.dot(pick[low], rows, preferred_element_type=F32).astype(BF16)
        give_out[low] = jnp.dot(other[low], rows, preferred_element_type=F32).astype(BF16)
    for out, core in ((keep_out, c), (give_out, 1 - c)):
        low = pl.multiple_of((2 * x + core) * TOK, TOK)
        for k in range(4):
            out[8 * CAP :, k * 128 : k * 128 + 128] = heads[k, pl.ds(low, TOK), :]


def expert_kernel(meta, keep, got, wo_all, rows, tokens, gain, own, other, given_a, given_b,
                  mid_out, out, raw, wide, deep, sems):
    zh, c = meta[2], meta[4]

    @pl.when(c == zh)
    def _():
        pltpu.make_async_copy(own, raw.at[0], sems.at[0]).start()
        pltpu.make_async_copy(given_a, raw.at[1], sems.at[1]).start()

    @pl.when(c != zh)
    def _():
        pltpu.make_async_copy(other, raw.at[0], sems.at[0]).start()
        pltpu.make_async_copy(given_b, raw.at[1], sems.at[1]).start()

    tiles = []
    for k in range(4):
        one = keep[:, k * 128 : k * 128 + 128]
        two = got[:, k * 128 : k * 128 + 128]
        tiles += [jnp.where(c == 0, one, two), jnp.where(c == 0, two, one)]
    total = jnp.dot(jnp.concatenate(tiles, axis=1), wo_all[...], preferred_element_type=F32)
    mid_out[...] = (tokens[...].astype(F32) + total[8 * CAP :]).astype(BF16)
    mid = (rows[...].astype(F32) + total[: 8 * CAP]).astype(BF16)
    arrived = rms(mid.astype(F32), gain[...])
    acts = []
    for half, source in enumerate((own, given_a)):
        pltpu.make_async_copy(source, raw.at[half], sems.at[half]).wait()
        for e in range(8):
            low = e * 288
            wide[half, e * 192 : e * 192 + 192] = raw[half, low : low + 192]
            for i in range(3):
                deep[half, i * 256 + e * 32 : i * 256 + e * 32 + 32] = raw[
                    half, low + 192 + 32 * i : low + 224 + 32 * i
                ]
        both = jnp.dot(arrived, wide[half], preferred_element_type=F32)
        gate, up = both[:, :256], both[:, 256:]
        acts.append((gate / (1.0 + jnp.exp(-gate)) * up).astype(BF16))
    for i in range(3):
        chunk = slice(i * 256, i * 256 + 256)
        total = jnp.dot(acts[0], deep[0, chunk], preferred_element_type=F32)
        total += jnp.dot(acts[1], deep[1, chunk], preferred_element_type=F32)
        out[:, i * 512 : i * 512 + 512] = total.astype(BF16)


def combine_kernel(returned, mid, slots, weights, out):
    total = mid[...].astype(F32)
    for k in range(2):
        pick = choose(slots, k).astype(F32).astype(BF16)
        chosen = dot_tn(pick, returned[...])
        total += chosen * column(weights[k : k + 1])[:, 0:1]
    out[...] = total.astype(BF16)


def body(
    tokens,
    attn_gain,
    ffn_gain,
    w_query,
    key_value_weight,
    w_out,
    segment_ids,
    expert_ids,
    route_weights,
    w_gate,
    w_up,
    w_down,
    page_table,
):
    y, zq, zp, zh, x, c = (lax.axis_index(name) for name in AXES)
    zl = zq * 2 + zp
    place = (((y * 8 + zl) * 2 + zh) * 4 + x) * 2 + c
    meta = jnp.stack([y, zl, zh, x, c, place]).astype(I32)
    wq, wkv = w_query.T, key_value_weight.T
    ids = expert_ids.T

    parts = jnp.concatenate(
        [lax.dynamic_slice_in_dim(w, y * 16, 16, 0) for w in (wq, wkv, w_out)], axis=0
    )
    parts = swap_half(parts)
    (block,) = call(
        pack_kernel, [((4, TOK + 16, WIDTH), BF16)], [SMEM] + [VMEM] * 3, nbytes=0
    )(meta, tokens, segment_ids[None, :], ids)
    (eighth,) = call(
        eighth_kernel,
        [((288, 512), BF16)],
        [SMEM] + [ANY] * 3,
        scratch=[pltpu.SemaphoreType.DMA((5,))],
        nbytes=0,
    )(meta, w_gate, w_up, w_down)
    near = lax.all_to_all(block, "x", split_axis=0, concat_axis=0, tiled=True)
    eighth = swap_half(eighth)
    near, parts, eighth = lax.optimization_barrier((near, parts, eighth))
    parts = gather(parts, "y").reshape(4, 3, 16, WIDTH)
    far_cols = parts[:, :2].transpose(1, 0, 2, 3).reshape(128, WIDTH)
    across = swap_core(near)
    gain = attn_gain[None, :]
    q, kv, start = call(
        project_kernel,
        [((ROWS, 128), BF16), ((ROWS, 128), BF16), ((ROWS, 128), F32)],
        [SMEM] + [VMEM] * 6,
        scratch=[pltpu.VMEM((256, WIDTH), BF16)],
        flops=0,
        nbytes=0,
    )(meta, near, across, wq, wkv, far_cols, gain)
    out_rows = jnp.concatenate([w_out, parts[:, 2].reshape(64, WIDTH)], axis=0)
    out_all = lax.all_gather(out_rows, ROW, axis=0, tiled=True)

    partner = swap_half(kv)
    sums, maxes, dens, slots = call(
        own_kernel,
        [((ROWS, 128), F32)] * 3 + [((8, TOK), I32)],
        [VMEM] * 4,
        scratch=[pltpu.VMEM((ROWS, 128), BF16)] * 2,
        flops=0,
        nbytes=0,
    )(q, kv, start, ids)
    pick, other_pick, chosen = call(
        route_kernel,
        [((8 * CAP, TOK), BF16)] * 2 + [((8 * CAP, WIDTH), BF16)],
        [SMEM] + [VMEM] * 2,
        flops=0,
        nbytes=0,
    )(meta, after(near, sums), across)

    (own,) = call(order_kernel, [((2304, 512), BF16)], [VMEM] * 3, nbytes=0)(
        *(after(w, sums) for w in (w_gate, w_up, w_down))
    )
    given_a = give_half(own, True)
    other = gather(after(eighth, sums), ("y", "zp")).reshape(2304, 512)

    shifted = next_group(jnp.where(zh == 0, partner, kv))
    (pages,) = call(
        page_kernel,
        [((ROWS, 128), BF16)],
        [SMEM, SMEM] + [VMEM] * 2,
        scratch=[pltpu.VMEM((2 * ROWS, 128), BF16)],
        nbytes=0,
    )(meta, page_table, kv, partner)
    held = lax.all_to_all(
        pages.reshape(8, TOK, 128), ROW, split_axis=0, concat_axis=0, tiled=True
    )
    previous = jnp.where(zh == 0, shifted, partner)
    (heads,) = call(
        before_kernel,
        [((4, ROWS, 128), BF16)],
        [VMEM] * 6,
        scratch=[pltpu.VMEM((ROWS, 128), BF16)] * 2,
        flops=0,
        nbytes=0,
    )(after(q, pages), previous, start, sums, maxes, dens)
    other = after(other, heads)
    given_b = give_half(other, False)
    heads = lax.all_to_all(heads, "x", split_axis=0, concat_axis=0, tiled=True)
    (cache,) = call(cache_kernel, [((TOK, 1024), BF16)], [VMEM], nbytes=0)(held)
    keep, give = call(
        split_kernel,
        [((4 * TOK, 512), BF16)] * 2,
        [SMEM] + [VMEM] * 3,
        flops=0,
        nbytes=0,
    )(meta, heads, pick, other_pick)
    got = swap_core(give)
    mid, expert_out = call(
        expert_kernel,
        [((TOK, WIDTH), BF16), ((8 * CAP, WIDTH), BF16)],
        [SMEM] + [VMEM] * 6 + [ANY] * 4,
        scratch=[
            pltpu.VMEM((2, 2304, 512), BF16),
            pltpu.VMEM((2, WIDTH, 512), BF16),
            pltpu.VMEM((2, 768, 512), BF16),
            pltpu.SemaphoreType.DMA((2,)),
        ],
        flops=0,
        nbytes=0,
    )(meta, keep, got, out_all, chosen, tokens, ffn_gain[None, :], own, other, given_a, given_b)
    returned = lax.all_to_all(
        expert_out.reshape(8, CAP, WIDTH), ROW, split_axis=0, concat_axis=0, tiled=True
    ).reshape(8 * CAP, WIDTH)
    (hidden,) = call(
        combine_kernel, [((TOK, WIDTH), BF16)], [VMEM] * 4, flops=0, nbytes=0
    )(returned, mid, slots, route_weights.T)
    return (hidden, cache.reshape(8, PAGE, 1024))


def solution(mesh):
    fine = Mesh(mesh.devices.reshape(SIZES), AXES)
    grp, tp = ("y", "zq", "zp"), ("zh", "x", "c")
    in_specs = (
        P(AXES, None),
        P(),
        P(),
        P(None, tp),
        P(None, tp),
        P(tp, None),
        P(AXES),
        P(AXES, None),
        P(AXES, None),
        P(None, tp),
        P(None, tp),
        P(tp, None),
        P(grp, None),
    )
    out_specs = (P(AXES, None), P(AXES, None, None))
    return jax.shard_map(body, mesh=fine, in_specs=in_specs, out_specs=out_specs, check_vma=False)
```

```python
import functools

import jax
import jax.numpy as jnp
import numpy as np
from jax import lax
from jax.experimental import pallas as pl
from jax.experimental.pallas import tpu as pltpu
from jax.sharding import Mesh
from jax.sharding import PartitionSpec as P

AXES = ("y", "zq", "zr", "zp", "zh", "x", "c")
SIZES = (4, 2, 2, 2, 2, 4, 2)
FLAT = (4, 8, 2, 4, 2)
ROW = ("x", "c")
PAGE = 16
CAP = 48
TOK = 128
WIDTH = 1536
ROWS = 8 * TOK
BF16 = jnp.bfloat16
F32 = jnp.float32
I32 = jnp.int32
VMEM = pl.BlockSpec(memory_space=pltpu.VMEM)
ANY = pl.BlockSpec(memory_space=pl.ANY)
SMEM = pl.BlockSpec(memory_space=pltpu.SMEM)
MIB = 1 << 20


def permute(block, target):
    route = []
    for source in range(int(np.prod(FLAT))):
        goal = target(*(int(v) for v in np.unravel_index(source, FLAT)))
        if goal is not None:
            route.append((source, int(np.ravel_multi_index(goal, FLAT))))
    return lax.ppermute(block, AXES, route)


def swap_core(block):
    return permute(block, lambda y, zl, zh, x, c: (y, zl, zh, x, 1 - c))


def swap_half(block):
    return permute(block, lambda y, zl, zh, x, c: (y, zl, 1 - zh, x, c))


def swap_near(block):
    return permute(block, lambda y, zl, zh, x, c: (y, zl ^ 1, zh, x, c))


def next_group(block):
    def target(y, zl, zh, x, c):
        if zl < 7:
            return (y, zl + 1, 0, x, c) if zh == 0 else None
        return (y + 1, 0, 0, x, c) if zh == 1 and y < 3 else None

    return permute(block, target)


def ahead_x(block, step):
    return permute(block, lambda y, zl, zh, x, c: (y, zl, zh, (x - step) % 4, c))


def give_half(block, near):
    def target(y, zl, zh, x, c):
        return (y, zl, zh, x, 1 - c) if (c == zh) != near else None

    return permute(block, target)


def gather(block, axis):
    wide = jnp.broadcast_to(block[None], (lax.axis_size(axis),) + block.shape)
    return lax.all_to_all(wide, axis, split_axis=0, concat_axis=0, tiled=True)


def after(value, *earlier):
    return lax.optimization_barrier((value,) + earlier)[0]


def call(kernel, outs, in_specs, scratch=(), flops=0, nbytes=0, limit=48):
    outs = [jax.ShapeDtypeStruct(shape, kind) for shape, kind in outs]
    return pl.pallas_call(
        kernel,
        out_shape=outs,
        in_specs=in_specs,
        out_specs=[VMEM] * len(outs),
        scratch_shapes=list(scratch),
        compiler_params=pltpu.CompilerParams(vmem_limit_bytes=limit * MIB),
        cost_estimate=pl.CostEstimate(flops=flops, bytes_accessed=nbytes, transcendentals=0),
    )


def dot_nt(left, right):
    return lax.dot_general(left, right, (((1,), (1,)), ((), ())), preferred_element_type=F32)


def dot_tn(left, right):
    return lax.dot_general(left, right, (((0,), (0,)), ((), ())), preferred_element_type=F32)


def column(lane_row):
    return jnp.transpose(jnp.broadcast_to(lane_row, (TOK, TOK)))


def rms(values, gain):
    inverse = lax.rsqrt(jnp.mean(values * values, axis=-1, keepdims=True) + 1e-05)
    return (values * inverse * gain).astype(BF16)


def pack_kernel(meta, tokens, seg, ids, out):
    own = meta[5] * TOK + lax.broadcasted_iota(I32, (1, TOK), 1)
    back = own - seg[...]
    row = lax.broadcasted_iota(I32, (16, TOK), 0)
    pieces = jnp.where(row == 0, back >> 5, jnp.where(row == 1, back & 31, 0))
    pieces = jnp.where(row == 2, ids[0:1], jnp.where(row == 3, ids[1:2], pieces))
    pieces = pieces.astype(F32).astype(BF16)
    out[:TOK] = tokens[...]
    out[TOK:, :TOK] = pieces
    out[TOK:, TOK:] = jnp.zeros((16, WIDTH - TOK), BF16)


def piece_kernel(meta, gate, up, down, out, sems):
    piece = meta[0] * 4 + lax.rem(meta[1], 4)
    wide = pl.ds(pl.multiple_of(piece * 96, 32), 96)
    deep = pl.ds(pl.multiple_of(piece * 16, 16), 16)
    copies = [
        pltpu.make_async_copy(gate.at[wide], out.at[:96, :256], sems.at[0]),
        pltpu.make_async_copy(up.at[wide], out.at[:96, 256:], sems.at[1]),
    ]
    for i in range(3):
        copies.append(
            pltpu.make_async_copy(
                down.at[deep, i * 512 : i * 512 + 512],
                out.at[96 + 16 * i : 112 + 16 * i],
                sems.at[2 + i],
            )
        )
    for copy in copies:
        copy.start()
    for copy in copies:
        copy.wait()


def order_kernel(gate, up, down, out):
    for e in range(16):
        low = e * 144
        out[low : low + 96, :256] = gate[e * 96 : e * 96 + 96]
        out[low : low + 96, 256:] = up[e * 96 : e * 96 + 96]
        for i in range(3):
            out[low + 96 + 16 * i : low + 112 + 16 * i] = down[
                e * 16 : e * 16 + 16, i * 512 : i * 512 + 512
            ]


def project_kernel(meta, b0, b1, b2, b3, s0, s1, s2, s3, wq, wkv, far, gain,
                   q_out, kv_out, start_out, cols):
    zh, x, c = meta[2], meta[3], meta[4]
    cols[0:64] = wq[...]
    cols[64:128] = far[0:64]
    cols[pl.ds(pl.multiple_of(128 + zh * 64, 64), 64), :] = wkv[...]
    cols[pl.ds(pl.multiple_of(192 - zh * 64, 64), 64), :] = far[64:128]
    for k in range(4):
        place = lax.rem(x + k, 4) * 2
        for block, core in (((b0, b1, b2, b3)[k], c), ((s0, s1, s2, s3)[k], 1 - c)):
            low = pl.multiple_of((place + core) * TOK, TOK)
            normed = rms(block[:TOK].astype(F32), gain[...])
            result = dot_nt(normed, cols[...]).astype(BF16)
            q_out[pl.ds(low, TOK), :] = result[:, :128]
            kv_out[pl.ds(low, TOK), :] = result[:, 128:]
            pieces = block[TOK:, :TOK].astype(F32)
            back = column(pieces[0:1] * 32.0 + pieces[1:2])
            own = (low + lax.broadcasted_iota(I32, (TOK, TOK), 0)).astype(F32)
            start_out[pl.ds(low, TOK), :] = own - back


def route_kernel(meta, b0, b1, b2, b3, s0, s1, s2, s3, pick_out, other_out, rows_out):
    x, c = meta[3], meta[4]
    before = lax.broadcasted_iota(I32, (TOK, TOK), 0) < lax.broadcasted_iota(I32, (TOK, TOK), 1)
    before = before.astype(F32).astype(BF16)
    row = lax.broadcasted_iota(I32, (CAP, TOK), 0).astype(F32)
    for expert, out in ((x + 4 * c, pick_out), (x + 4 * (1 - c), other_out)):
        number = expert.astype(F32)
        for k in range(4):
            place = lax.rem(x + k, 4) * 2
            for block, core in (((b0, b1, b2, b3)[k], c), ((s0, s1, s2, s3)[k], 1 - c)):
                low = pl.multiple_of((place + core) * CAP, 16)
                pieces = block[TOK:, :TOK].astype(F32)
                named = (pieces == number).astype(F32)
                named = named[2:3] + named[3:4]
                rank = jnp.dot(
                    jnp.broadcast_to(named, (8, TOK)).astype(BF16),
                    before,
                    preferred_element_type=F32,
                )[0:1]
                pick = jnp.where((row == rank) & (named > 0.0), 1.0, 0.0).astype(BF16)
                out[pl.ds(low, CAP), :] = pick
                if out is pick_out:
                    chosen = jnp.dot(pick, block[:TOK], preferred_element_type=F32)
                    rows_out[pl.ds(low, CAP), :] = chosen.astype(BF16)


def split_kv(kv):
    wide = kv[...].astype(F32)
    turned = pltpu.roll(wide, 64, 1)
    low = lax.broadcasted_iota(I32, wide.shape, 1) < 64
    return (
        jnp.where(low, wide, turned).astype(BF16),
        jnp.where(low, turned, wide).astype(BF16),
    )


STEP = 256


def own_kernel(q, kv, start, ids, sum_out, max_out, den_out, slots_out, keys, values):
    keys[...], values[...] = split_kv(kv)
    low_lane = lax.broadcasted_iota(I32, (STEP, 128), 1) < 64
    for block in range(ROWS // STEP):
        low = block * STEP
        span = low + STEP
        query = q[low:span]
        position = lax.broadcasted_iota(I32, (STEP, span), 1).astype(F32)
        own = (low + lax.broadcasted_iota(I32, (STEP, span), 0)).astype(F32)
        allowed = (position <= own) & (position >= start[low:span, 0:1])
        parts = []
        for head in range(2):
            kept = jnp.where(low_lane if head == 0 else ~low_lane, query, jnp.zeros_like(query))
            scores = jnp.where(allowed, dot_nt(kept, keys[:span]) * 0.125, -1e30)
            top = jnp.max(scores, axis=-1, keepdims=True)
            weights = jnp.exp(scores - top)
            den = jnp.sum(weights, axis=-1, keepdims=True)
            part = jnp.dot(weights.astype(BF16), values[:span], preferred_element_type=F32)
            parts.append((part, top, den))
        for out, one, two in zip((sum_out, max_out, den_out), *parts):
            out[low:span] = jnp.where(low_lane, one, two)
    choice = [ids[k : k + 1].astype(F32) for k in range(2)]
    down = [column(v) for v in choice]
    earlier = lax.broadcasted_iota(I32, (TOK, TOK), 0) < lax.broadcasted_iota(I32, (TOK, TOK), 1)
    result = []
    for k in range(2):
        same = sum((down[j] == choice[k]).astype(F32) for j in range(2))
        rank = jnp.sum(jnp.where(earlier, same, 0.0), axis=0, keepdims=True).astype(I32)
        expert = ids[k : k + 1]
        result.append(((expert & 3) * 2 + (expert >> 2)) * CAP + rank)
    row = lax.broadcasted_iota(I32, (8, TOK), 0)
    slots_out[...] = jnp.where(row == 0, result[0], result[1])


def before_kernel(q, kv, start, sums, maxes, dens, out, keys, values):
    keys[...], values[...] = split_kv(kv)
    low_lane = lax.broadcasted_iota(I32, (STEP, 128), 1) < 64
    for block in range(ROWS // STEP):
        low = block * STEP
        high = low + STEP
        span = ROWS - low
        query = q[low:high]
        position = (low - ROWS + lax.broadcasted_iota(I32, (STEP, span), 1)).astype(F32)
        allowed = position >= start[low:high, 0:1]
        parts = []
        for head in range(2):
            kept = jnp.where(low_lane if head == 0 else ~low_lane, query, jnp.zeros_like(query))
            scores = jnp.where(allowed, dot_nt(kept, keys[low:]) * 0.125, -1e30)
            first = maxes[low:high, head * 64 : head * 64 + 1]
            top = jnp.maximum(first, jnp.max(scores, axis=-1, keepdims=True))
            weights = jnp.exp(scores - top)
            scale = jnp.exp(first - top)
            den = jnp.sum(weights, axis=-1, keepdims=True)
            part = jnp.dot(weights.astype(BF16), values[low:], preferred_element_type=F32)
            parts.append((part, scale, den))
        part, scale, den = (jnp.where(low_lane, one, two) for one, two in zip(*parts))
        total = sums[low:high] * scale + part
        result = (total / (dens[low:high] * scale + den)).astype(BF16)
        for copy in range(4):
            out[copy, low:high, :] = result


def page_kernel(meta, table, kv, partner, out, group):
    zh = meta[2]
    group[pl.ds(pl.multiple_of(zh * ROWS, ROWS), ROWS), :] = kv[...]
    group[pl.ds(pl.multiple_of((1 - zh) * ROWS, ROWS), ROWS), :] = partner[...]

    def place(block, carry):
        page = table[0, block] - zh * 64

        @pl.when((page >= 0) & (page < 64))
        def _():
            out[pl.ds(pl.multiple_of(page * PAGE, PAGE), PAGE), :] = group[
                pl.ds(pl.multiple_of(block * PAGE, PAGE), PAGE), :
            ]

        return carry

    lax.fori_loop(0, 128, place, 0)


def cache_kernel(pages, out):
    low = lax.broadcasted_iota(I32, (TOK, 128), 1) < 64
    for pair in range(4):
        one = pages[2 * pair].astype(F32)
        two = pages[2 * pair + 1].astype(F32)
        lanes = slice(pair * 128, pair * 128 + 128)
        out[:, lanes] = jnp.where(low, one, pltpu.roll(two, 64, 1)).astype(BF16)
        lanes = slice(512 + pair * 128, 640 + pair * 128)
        out[:, lanes] = jnp.where(low, pltpu.roll(one, 64, 1), two).astype(BF16)


def choose(slots, k):
    place = lax.broadcasted_iota(I32, (8 * CAP, TOK), 0)
    return place == slots[k : k + 1]


def split_kernel(meta, heads, pick, other, keep_out, give_out):
    x, c = meta[3], meta[4]
    for d in range(8):
        rows = jnp.concatenate([heads[k, d * TOK : d * TOK + TOK] for k in range(4)], axis=1)
        low = slice(d * CAP, d * CAP + CAP)
        keep_out[low] = jnp.dot(pick[low], rows, preferred_element_type=F32).astype(BF16)
        give_out[low] = jnp.dot(other[low], rows, preferred_element_type=F32).astype(BF16)
    for out, core in ((keep_out, c), (give_out, 1 - c)):
        low = pl.multiple_of((2 * x + core) * TOK, TOK)
        for k in range(4):
            out[8 * CAP :, k * 128 : k * 128 + 128] = heads[k, pl.ds(low, TOK), :]


def expert_kernel(meta, keep, got, wo_all, rows, tokens, gain, own, other, given_a, given_b,
                  mid_out, out, raw, wide, deep, sems):
    zh, c = meta[2], meta[4]

    @pl.when(c == zh)
    def _():
        pltpu.make_async_copy(own, raw.at[0], sems.at[0]).start()
        pltpu.make_async_copy(given_a, raw.at[1], sems.at[1]).start()

    @pl.when(c != zh)
    def _():
        pltpu.make_async_copy(other, raw.at[0], sems.at[0]).start()
        pltpu.make_async_copy(given_b, raw.at[1], sems.at[1]).start()

    tiles = []
    for k in range(4):
        one = keep[:, k * 128 : k * 128 + 128]
        two = got[:, k * 128 : k * 128 + 128]
        tiles += [jnp.where(c == 0, one, two), jnp.where(c == 0, two, one)]
    total = jnp.dot(jnp.concatenate(tiles, axis=1), wo_all[...], preferred_element_type=F32)
    mid_out[...] = (tokens[...].astype(F32) + total[8 * CAP :]).astype(BF16)
    mid = (rows[...].astype(F32) + total[: 8 * CAP]).astype(BF16)
    arrived = rms(mid.astype(F32), gain[...])
    acts = []
    for half, source in enumerate((own, given_a)):
        pltpu.make_async_copy(source, raw.at[half], sems.at[half]).wait()
        for e in range(16):
            low = e * 144
            wide[half, e * 96 : e * 96 + 96] = raw[half, low : low + 96]
            for i in range(3):
                deep[half, i * 256 + e * 16 : i * 256 + e * 16 + 16] = raw[
                    half, low + 96 + 16 * i : low + 112 + 16 * i
                ]
        both = jnp.dot(arrived, wide[half], preferred_element_type=F32)
        gate, up = both[:, :256], both[:, 256:]
        acts.append((gate / (1.0 + jnp.exp(-gate)) * up).astype(BF16))
    for i in range(3):
        chunk = slice(i * 256, i * 256 + 256)
        total = jnp.dot(acts[0], deep[0, chunk], preferred_element_type=F32)
        total += jnp.dot(acts[1], deep[1, chunk], preferred_element_type=F32)
        out[:, i * 512 : i * 512 + 512] = total.astype(BF16)


def combine_kernel(returned, mid, slots, weights, out):
    total = mid[...].astype(F32)
    for k in range(2):
        pick = choose(slots, k).astype(F32).astype(BF16)
        chosen = dot_tn(pick, returned[...])
        total += chosen * column(weights[k : k + 1])[:, 0:1]
    out[...] = total.astype(BF16)


def body(
    tokens,
    attn_gain,
    ffn_gain,
    w_query,
    key_value_weight,
    w_out,
    segment_ids,
    expert_ids,
    route_weights,
    w_gate,
    w_up,
    w_down,
    page_table,
):
    y, zq, zr, zp, zh, x, c = (lax.axis_index(name) for name in AXES)
    zl = zq * 4 + zr * 2 + zp
    place = (((y * 8 + zl) * 2 + zh) * 4 + x) * 2 + c
    meta = jnp.stack([y, zl, zh, x, c, place]).astype(I32)
    wq, wkv = w_query.T, key_value_weight.T
    ids = expert_ids.T

    parts = jnp.concatenate(
        [lax.dynamic_slice_in_dim(w, y * 16, 16, 0) for w in (wq, wkv, w_out)], axis=0
    )
    parts = swap_half(parts)
    (block,) = call(
        pack_kernel, [((TOK + 16, WIDTH), BF16)], [SMEM] + [VMEM] * 3, nbytes=0
    )(meta, tokens, segment_ids[None, :], ids)
    (piece,) = call(
        piece_kernel,
        [((144, 512), BF16)],
        [SMEM] + [ANY] * 3,
        scratch=[pltpu.SemaphoreType.DMA((5,))],
        nbytes=0,
    )(meta, w_gate, w_up, w_down)
    one, three, two = [ahead_x(block, step) for step in (1, 3, 2)]
    piece = swap_half(piece)
    one, two, three, parts, piece = lax.optimization_barrier((one, two, three, parts, piece))
    parts = gather(parts, "y").reshape(4, 3, 16, WIDTH)
    far_cols = parts[:, :2].transpose(1, 0, 2, 3).reshape(128, WIDTH)
    near = [block, one, two, three]
    across = [swap_core(b) for b in near]
    beside = swap_near(piece)
    gain, beside = lax.optimization_barrier((attn_gain[None, :], beside))
    q, kv, start = call(
        project_kernel,
        [((ROWS, 128), BF16), ((ROWS, 128), BF16), ((ROWS, 128), F32)],
        [SMEM] + [VMEM] * 12,
        scratch=[pltpu.VMEM((256, WIDTH), BF16)],
        flops=0,
        nbytes=0,
    )(meta, *near, *across, wq, wkv, far_cols, gain)
    out_rows = jnp.concatenate([w_out, parts[:, 2].reshape(64, WIDTH)], axis=0)
    out_all = lax.all_gather(out_rows, ROW, axis=0, tiled=True)

    partner = swap_half(kv)
    sums, maxes, dens, slots = call(
        own_kernel,
        [((ROWS, 128), F32)] * 3 + [((8, TOK), I32)],
        [VMEM] * 4,
        scratch=[pltpu.VMEM((ROWS, 128), BF16)] * 2,
        flops=4000000000,
        nbytes=3000000,
    )(q, kv, start, ids)
    pick, other_pick, chosen = call(
        route_kernel,
        [((8 * CAP, TOK), BF16)] * 2 + [((8 * CAP, WIDTH), BF16)],
        [SMEM] + [VMEM] * 8,
        flops=2000000000,
        nbytes=5000000,
    )(meta, after(block, kv), *near[1:], *across)

    (own,) = call(order_kernel, [((2304, 512), BF16)], [VMEM] * 3, nbytes=5000000)(
        *(after(w, kv) for w in (w_gate, w_up, w_down))
    )
    pair = jnp.where(
        zp == 0,
        jnp.concatenate([piece, beside], axis=0),
        jnp.concatenate([beside, piece], axis=0),
    )
    partner, sums, pick, own, out_all, pair = lax.optimization_barrier(
        (partner, sums, pick, own, out_all, pair)
    )
    onward = jnp.where(zh == 0, partner, kv)
    shifted = next_group(onward)
    given_a = give_half(own, True)
    other = gather(pair, ("y", "zr")).reshape(2304, 512)
    (pages,) = call(
        page_kernel,
        [((ROWS, 128), BF16)],
        [SMEM, SMEM] + [VMEM] * 2,
        scratch=[pltpu.VMEM((2 * ROWS, 128), BF16)],
        nbytes=0,
    )(meta, page_table, kv, partner)
    held = lax.all_to_all(
        pages.reshape(8, TOK, 128), ROW, split_axis=0, concat_axis=0, tiled=True
    )
    previous = jnp.where(zh == 0, shifted, partner)
    (heads,) = call(
        before_kernel,
        [((4, ROWS, 128), BF16)],
        [VMEM] * 6,
        scratch=[pltpu.VMEM((ROWS, 128), BF16)] * 2,
        flops=0,
        nbytes=0,
    )(after(q, pages), previous, start, sums, maxes, dens)
    other = after(other, heads)
    given_b = give_half(other, False)
    heads = lax.all_to_all(heads, "x", split_axis=0, concat_axis=0, tiled=True)
    (cache,) = call(cache_kernel, [((TOK, 1024), BF16)], [VMEM], nbytes=0)(held)
    keep, give = call(
        split_kernel,
        [((4 * TOK, 512), BF16)] * 2,
        [SMEM] + [VMEM] * 3,
        flops=0,
        nbytes=0,
    )(meta, heads, pick, other_pick)
    got = swap_core(give)
    mid, expert_out = call(
        expert_kernel,
        [((TOK, WIDTH), BF16), ((8 * CAP, WIDTH), BF16)],
        [SMEM] + [VMEM] * 6 + [ANY] * 4,
        scratch=[
            pltpu.VMEM((2, 2304, 512), BF16),
            pltpu.VMEM((2, WIDTH, 512), BF16),
            pltpu.VMEM((2, 768, 512), BF16),
            pltpu.SemaphoreType.DMA((2,)),
        ],
        flops=0,
        nbytes=0,
    )(meta, keep, got, out_all, chosen, tokens, ffn_gain[None, :], own, other, given_a, given_b)
    returned = lax.all_to_all(
        expert_out.reshape(8, CAP, WIDTH), ROW, split_axis=0, concat_axis=0, tiled=True
    ).reshape(8 * CAP, WIDTH)
    (hidden,) = call(
        combine_kernel, [((TOK, WIDTH), BF16)], [VMEM] * 4, flops=0, nbytes=0
    )(returned, mid, slots, route_weights.T)
    return (hidden, cache.reshape(8, PAGE, 1024))


def solution(mesh):
    fine = Mesh(mesh.devices.reshape(SIZES), AXES)
    grp, tp = ("y", "zq", "zr", "zp"), ("zh", "x", "c")
    in_specs = (
        P(AXES, None),
        P(),
        P(),
        P(None, tp),
        P(None, tp),
        P(tp, None),
        P(AXES),
        P(AXES, None),
        P(AXES, None),
        P(None, tp),
        P(None, tp),
        P(tp, None),
        P(grp, None),
    )
    out_specs = (P(AXES, None), P(AXES, None, None))
    return jax.shard_map(body, mesh=fine, in_specs=in_specs, out_specs=out_specs, check_vma=False)
```

```python
import functools

import jax
import jax.numpy as jnp
import numpy as np
from jax import lax
from jax.experimental import pallas as pl
from jax.experimental.pallas import tpu as pltpu
from jax.sharding import Mesh
from jax.sharding import PartitionSpec as P

AXES = ("y", "zq", "zr", "zp", "zh", "x", "c")
SIZES = (4, 2, 2, 2, 2, 4, 2)
FLAT = (4, 8, 2, 4, 2)
ROW = ("x", "c")
PAGE = 16
CAP = 48
TOK = 128
WIDTH = 1536
ROWS = 8 * TOK
BF16 = jnp.bfloat16
F32 = jnp.float32
I32 = jnp.int32
VMEM = pl.BlockSpec(memory_space=pltpu.VMEM)
HBM = pl.BlockSpec(memory_space=pltpu.HBM)
SMEM = pl.BlockSpec(memory_space=pltpu.SMEM)
MIB = 1 << 20


def permute(block, target):
    route = []
    for source in range(int(np.prod(FLAT))):
        goal = target(*(int(v) for v in np.unravel_index(source, FLAT)))
        if goal is not None:
            route.append((source, int(np.ravel_multi_index(goal, FLAT))))
    return lax.ppermute(block, AXES, route)


def swap_core(block):
    return permute(block, lambda y, zl, zh, x, c: (y, zl, zh, x, 1 - c))


def swap_half(block):
    return permute(block, lambda y, zl, zh, x, c: (y, zl, 1 - zh, x, c))


def swap_near(block, step):
    return permute(block, lambda y, zl, zh, x, c: (y, zl ^ step, zh, x, c))


def in_pair(mine, theirs, place):
    first = jnp.where(place == 0, mine, theirs)
    return jnp.concatenate([first, jnp.where(place == 0, theirs, mine)], axis=0)


def next_group(block):
    def target(y, zl, zh, x, c):
        if zl < 7:
            return (y, zl + 1, 0, x, c) if zh == 0 else None
        return (y + 1, 0, 0, x, c) if zh == 1 and y < 3 else None

    return permute(block, target)


def give_half(block, near):
    def target(y, zl, zh, x, c):
        return (y, zl, zh, x, 1 - c) if (c == zh) != near else None

    return permute(block, target)


def gather(block, axis):
    wide = jnp.broadcast_to(block[None], (lax.axis_size(axis),) + block.shape)
    return lax.all_to_all(wide, axis, split_axis=0, concat_axis=0, tiled=True)


def after(value, *earlier):
    return lax.optimization_barrier((value,) + earlier)[0]


def call(kernel, outs, in_specs, scratch=(), flops=0, nbytes=0, limit=48):
    outs = [jax.ShapeDtypeStruct(shape, kind) for shape, kind in outs]
    return pl.pallas_call(
        kernel,
        out_shape=outs,
        in_specs=in_specs,
        out_specs=[VMEM] * len(outs),
        scratch_shapes=list(scratch),
        compiler_params=pltpu.CompilerParams(vmem_limit_bytes=limit * MIB),
        cost_estimate=pl.CostEstimate(flops=flops, bytes_accessed=nbytes, transcendentals=0),
    )


def dot_nt(left, right):
    return lax.dot_general(left, right, (((1,), (1,)), ((), ())), preferred_element_type=F32)


def dot_tn(left, right):
    return lax.dot_general(left, right, (((0,), (0,)), ((), ())), preferred_element_type=F32)


def column(lane_row):
    return jnp.transpose(jnp.broadcast_to(lane_row, (TOK, TOK)))


def rms(values, gain):
    inverse = lax.rsqrt(jnp.mean(values * values, axis=-1, keepdims=True) + 1e-05)
    return (values * inverse * gain).astype(BF16)


def pack_kernel(meta, tokens, seg, ids, out):
    own = meta[5] * TOK + lax.broadcasted_iota(I32, (1, TOK), 1)
    back = own - seg[...]
    row = lax.broadcasted_iota(I32, (16, TOK), 0)
    pieces = jnp.where(row == 0, back >> 5, jnp.where(row == 1, back & 31, 0))
    pieces = jnp.where(row == 2, ids[0:1], jnp.where(row == 3, ids[1:2], pieces))
    pieces = pieces.astype(F32).astype(BF16)
    for copy in range(4):
        out[copy, :TOK] = tokens[...]
        out[copy, TOK:, :TOK] = pieces
        out[copy, TOK:, TOK:] = jnp.zeros((16, WIDTH - TOK), BF16)


def piece_kernel(meta, gate, up, down, out, sems):
    place = lax.rem(meta[1], 4)
    piece = meta[0] * 4 + lax.rem(place, 2) * 2 + place // 2
    wide = pl.ds(pl.multiple_of(piece * 96, 32), 96)
    deep = pl.ds(pl.multiple_of(piece * 16, 16), 16)
    copies = [
        pltpu.make_async_copy(gate.at[wide], out.at[:96, :256], sems.at[0]),
        pltpu.make_async_copy(up.at[wide], out.at[:96, 256:], sems.at[1]),
    ]
    for i in range(3):
        copies.append(
            pltpu.make_async_copy(
                down.at[deep, i * 512 : i * 512 + 512],
                out.at[96 + 16 * i : 112 + 16 * i],
                sems.at[2 + i],
            )
        )
    for copy in copies:
        copy.start()
    for copy in copies:
        copy.wait()


def order_kernel(gate, up, down, out):
    for e in range(16):
        low = e * 144
        out[low : low + 96, :256] = gate[e * 96 : e * 96 + 96]
        out[low : low + 96, 256:] = up[e * 96 : e * 96 + 96]
        for i in range(3):
            out[low + 96 + 16 * i : low + 112 + 16 * i] = down[
                e * 16 : e * 16 + 16, i * 512 : i * 512 + 512
            ]


def project_kernel(meta, near, across, wq, wkv, far, gain,
                   q_out, kv_out, start_out, cols):
    zh, c = meta[2], meta[4]
    cols[0:64] = wq[...]
    cols[64:128] = far[0:64]
    cols[pl.ds(pl.multiple_of(128 + zh * 64, 64), 64), :] = wkv[...]
    cols[pl.ds(pl.multiple_of(192 - zh * 64, 64), 64), :] = far[64:128]
    for k in range(4):
        for block, core in ((near, c), (across, 1 - c)):
            low = pl.multiple_of((2 * k + core) * TOK, TOK)
            normed = rms(block[k, :TOK].astype(F32), gain[...])
            result = dot_nt(normed, cols[...]).astype(BF16)
            q_out[pl.ds(low, TOK), :] = result[:, :128]
            kv_out[pl.ds(low, TOK), :] = result[:, 128:]
            pieces = block[k, TOK:, :TOK].astype(F32)
            back = column(pieces[0:1] * 32.0 + pieces[1:2])
            own = (low + lax.broadcasted_iota(I32, (TOK, TOK), 0)).astype(F32)
            start_out[pl.ds(low, TOK), :] = own - back


def route_kernel(meta, near, across, pick_out, other_out, rows_out):
    x, c = meta[3], meta[4]
    before = lax.broadcasted_iota(I32, (TOK, TOK), 0) < lax.broadcasted_iota(I32, (TOK, TOK), 1)
    before = before.astype(F32).astype(BF16)
    row = lax.broadcasted_iota(I32, (CAP, TOK), 0).astype(F32)
    for expert, out in ((x + 4 * c, pick_out), (x + 4 * (1 - c), other_out)):
        number = expert.astype(F32)
        for k in range(4):
            for block, core in ((near, c), (across, 1 - c)):
                low = pl.multiple_of((2 * k + core) * CAP, 16)
                pieces = block[k, TOK:, :TOK].astype(F32)
                named = (pieces == number).astype(F32)
                named = named[2:3] + named[3:4]
                rank = jnp.dot(
                    jnp.broadcast_to(named, (8, TOK)).astype(BF16),
                    before,
                    preferred_element_type=F32,
                )[0:1]
                pick = jnp.where((row == rank) & (named > 0.0), 1.0, 0.0).astype(BF16)
                out[pl.ds(low, CAP), :] = pick
                if out is pick_out:
                    chosen = jnp.dot(pick, block[k, :TOK], preferred_element_type=F32)
                    rows_out[pl.ds(low, CAP), :] = chosen.astype(BF16)


def split_kv(kv):
    wide = kv[...].astype(F32)
    turned = pltpu.roll(wide, 64, 1)
    low = lax.broadcasted_iota(I32, wide.shape, 1) < 64
    return (
        jnp.where(low, wide, turned).astype(BF16),
        jnp.where(low, turned, wide).astype(BF16),
    )


STEP = 256


def own_kernel(q, kv, start, ids, sum_out, max_out, den_out, slots_out, keys, values):
    keys[...], values[...] = split_kv(kv)
    low_lane = lax.broadcasted_iota(I32, (STEP, 128), 1) < 64
    for block in range(ROWS // STEP):
        low = block * STEP
        span = low + STEP
        query = q[low:span]
        position = lax.broadcasted_iota(I32, (STEP, span), 1).astype(F32)
        own = (low + lax.broadcasted_iota(I32, (STEP, span), 0)).astype(F32)
        allowed = (position <= own) & (position >= start[low:span, 0:1])
        parts = []
        for head in range(2):
            kept = jnp.where(low_lane if head == 0 else ~low_lane, query, jnp.zeros_like(query))
            scores = jnp.where(allowed, dot_nt(kept, keys[:span]) * 0.125, -1e30)
            top = jnp.max(scores, axis=-1, keepdims=True)
            weights = jnp.exp(scores - top)
            den = jnp.sum(weights, axis=-1, keepdims=True)
            part = jnp.dot(weights.astype(BF16), values[:span], preferred_element_type=F32)
            parts.append((part, top, den))
        for out, one, two in zip((sum_out, max_out, den_out), *parts):
            out[low:span] = jnp.where(low_lane, one, two)
    choice = [ids[k : k + 1].astype(F32) for k in range(2)]
    down = [column(v) for v in choice]
    earlier = lax.broadcasted_iota(I32, (TOK, TOK), 0) < lax.broadcasted_iota(I32, (TOK, TOK), 1)
    result = []
    for k in range(2):
        same = sum((down[j] == choice[k]).astype(F32) for j in range(2))
        rank = jnp.sum(jnp.where(earlier, same, 0.0), axis=0, keepdims=True).astype(I32)
        expert = ids[k : k + 1]
        result.append(((expert & 3) * 2 + (expert >> 2)) * CAP + rank)
    row = lax.broadcasted_iota(I32, (8, TOK), 0)
    slots_out[...] = jnp.where(row == 0, result[0], result[1])


def before_kernel(q, kv, start, sums, maxes, dens, pages, out, keys, values):
    keys[...], values[...] = split_kv(kv)
    low_lane = lax.broadcasted_iota(I32, (STEP, 128), 1) < 64
    for block in range(ROWS // STEP):
        low = block * STEP
        high = low + STEP
        span = ROWS - low
        query = q[low:high]
        position = (low - ROWS + lax.broadcasted_iota(I32, (STEP, span), 1)).astype(F32)
        allowed = position >= start[low:high, 0:1]
        parts = []
        for head in range(2):
            kept = jnp.where(low_lane if head == 0 else ~low_lane, query, jnp.zeros_like(query))
            scores = jnp.where(allowed, dot_nt(kept, keys[low:]) * 0.125, -1e30)
            first = maxes[low:high, head * 64 : head * 64 + 1]
            top = jnp.maximum(first, jnp.max(scores, axis=-1, keepdims=True))
            weights = jnp.exp(scores - top)
            scale = jnp.exp(first - top)
            den = jnp.sum(weights, axis=-1, keepdims=True)
            part = jnp.dot(weights.astype(BF16), values[low:], preferred_element_type=F32)
            parts.append((part, scale, den))
        part, scale, den = (jnp.where(low_lane, one, two) for one, two in zip(*parts))
        total = sums[low:high] * scale + part
        result = (total / (dens[low:high] * scale + den)).astype(BF16)
        for copy in range(4):
            out[copy, low:high, :] = result
    for k in range(4):
        out[k, ROWS:, :] = pages[k * 256 : k * 256 + 256]


def page_kernel(meta, table, kv, partner, out, group):
    zh = meta[2]
    group[pl.ds(pl.multiple_of(zh * ROWS, ROWS), ROWS), :] = kv[...]
    group[pl.ds(pl.multiple_of((1 - zh) * ROWS, ROWS), ROWS), :] = partner[...]

    def place(block, carry):
        page = table[0, block] - zh * 64

        @pl.when((page >= 0) & (page < 64))
        def _():
            out[pl.ds(pl.multiple_of(page * PAGE, PAGE), PAGE), :] = group[
                pl.ds(pl.multiple_of(block * PAGE, PAGE), PAGE), :
            ]

        return carry

    lax.fori_loop(0, 128, place, 0)


def cache_kernel(meta, keep, got, out):
    c = meta[4]
    low = lax.broadcasted_iota(I32, (TOK, 128), 1) < 64
    for pair in range(4):
        lanes = slice(pair * 128, pair * 128 + 128)
        mine = keep[4 * TOK :, lanes].astype(F32)
        theirs = got[4 * TOK :, lanes].astype(F32)
        one = jnp.where(c == 0, mine, theirs)
        two = jnp.where(c == 0, theirs, mine)
        out[:, lanes] = jnp.where(low, one, pltpu.roll(two, 64, 1)).astype(BF16)
        lanes = slice(512 + pair * 128, 640 + pair * 128)
        out[:, lanes] = jnp.where(low, pltpu.roll(one, 64, 1), two).astype(BF16)


def choose(slots, k):
    place = lax.broadcasted_iota(I32, (8 * CAP, TOK), 0)
    return place == slots[k : k + 1]


def split_kernel(meta, heads, pick, other, keep_out, give_out):
    x, c = meta[3], meta[4]
    for d in range(8):
        rows = jnp.concatenate([heads[k, d * TOK : d * TOK + TOK] for k in range(4)], axis=1)
        low = slice(d * CAP, d * CAP + CAP)
        keep_out[low] = jnp.dot(pick[low], rows, preferred_element_type=F32).astype(BF16)
        give_out[low] = jnp.dot(other[low], rows, preferred_element_type=F32).astype(BF16)
    for out, core in ((keep_out, c), (give_out, 1 - c)):
        low = pl.multiple_of((2 * x + core) * TOK, TOK)
        page = pl.multiple_of(ROWS + core * TOK, TOK)
        for k in range(4):
            lanes = slice(k * 128, k * 128 + 128)
            out[8 * CAP : 4 * TOK, lanes] = heads[k, pl.ds(low, TOK), :]
            out[4 * TOK :, lanes] = heads[k, pl.ds(page, TOK), :]


def expert_kernel(meta, keep, got, wo_all, rows, tokens, gain, own, other, given_a, given_b,
                  mid_out, out, raw, wide, deep, sems):
    zh, c = meta[2], meta[4]

    @pl.when(c == zh)
    def _():
        pltpu.make_async_copy(own, raw.at[0], sems.at[0]).start()
        pltpu.make_async_copy(given_a, raw.at[1], sems.at[1]).start()

    @pl.when(c != zh)
    def _():
        pltpu.make_async_copy(other, raw.at[0], sems.at[0]).start()
        pltpu.make_async_copy(given_b, raw.at[1], sems.at[1]).start()

    tiles = []
    for k in range(4):
        one = keep[: 4 * TOK, k * 128 : k * 128 + 128]
        two = got[: 4 * TOK, k * 128 : k * 128 + 128]
        tiles += [jnp.where(c == 0, one, two), jnp.where(c == 0, two, one)]
    total = jnp.dot(jnp.concatenate(tiles, axis=1), wo_all[...], preferred_element_type=F32)
    mid_out[...] = (tokens[...].astype(F32) + total[8 * CAP :]).astype(BF16)
    mid = (rows[...].astype(F32) + total[: 8 * CAP]).astype(BF16)
    arrived = rms(mid.astype(F32), gain[...])
    acts = []
    for half, source in enumerate((own, given_a)):
        pltpu.make_async_copy(source, raw.at[half], sems.at[half]).wait()
        for e in range(16):
            low = e * 144
            wide[half, e * 96 : e * 96 + 96] = raw[half, low : low + 96]
            for i in range(3):
                deep[half, i * 256 + e * 16 : i * 256 + e * 16 + 16] = raw[
                    half, low + 96 + 16 * i : low + 112 + 16 * i
                ]
        both = jnp.dot(arrived, wide[half], preferred_element_type=F32)
        gate, up = both[:, :256], both[:, 256:]
        acts.append((gate / (1.0 + jnp.exp(-gate)) * up).astype(BF16))
    for i in range(3):
        chunk = slice(i * 256, i * 256 + 256)
        total = jnp.dot(acts[0], deep[0, chunk], preferred_element_type=F32)
        total += jnp.dot(acts[1], deep[1, chunk], preferred_element_type=F32)
        out[:, i * 512 : i * 512 + 512] = total.astype(BF16)


def combine_kernel(returned, mid, slots, weights, out):
    total = mid[...].astype(F32)
    for k in range(2):
        pick = choose(slots, k).astype(F32).astype(BF16)
        chosen = dot_tn(pick, returned[...])
        total += chosen * column(weights[k : k + 1])[:, 0:1]
    out[...] = total.astype(BF16)


def body(
    tokens,
    attn_gain,
    ffn_gain,
    w_query,
    key_value_weight,
    w_out,
    segment_ids,
    expert_ids,
    route_weights,
    w_gate,
    w_up,
    w_down,
    page_table,
):
    y, zq, zr, zp, zh, x, c = (lax.axis_index(name) for name in AXES)
    zl = zq * 4 + zr * 2 + zp
    place = (((y * 8 + zl) * 2 + zh) * 4 + x) * 2 + c
    meta = jnp.stack([y, zl, zh, x, c, place]).astype(I32)
    wq, wkv = w_query.T, key_value_weight.T
    ids = expert_ids.T

    parts = jnp.concatenate(
        [lax.dynamic_slice_in_dim(w, y * 16, 16, 0) for w in (wq, wkv, w_out)], axis=0
    )
    parts = swap_half(parts)
    (block,) = call(
        pack_kernel, [((4, TOK + 16, WIDTH), BF16)], [SMEM] + [VMEM] * 3, nbytes=0
    )(meta, tokens, segment_ids[None, :], ids)
    (piece,) = call(
        piece_kernel,
        [((144, 512), BF16)],
        [SMEM] + [HBM] * 3,
        scratch=[pltpu.SemaphoreType.DMA((5,))],
        nbytes=0,
    )(meta, w_gate, w_up, w_down)
    near = lax.all_to_all(block, "x", split_axis=0, concat_axis=0, tiled=True)
    piece = swap_half(piece)
    near, parts, piece = lax.optimization_barrier((near, parts, piece))
    parts = gather(parts, "y").reshape(4, 3, 16, WIDTH)
    far_cols = parts[:, :2].transpose(1, 0, 2, 3).reshape(128, WIDTH)
    across = swap_core(near)
    beside = swap_near(piece, 2)
    gain, beside = lax.optimization_barrier((attn_gain[None, :], beside))
    q, kv, start = call(
        project_kernel,
        [((ROWS, 128), BF16), ((ROWS, 128), BF16), ((ROWS, 128), F32)],
        [SMEM] + [VMEM] * 6,
        scratch=[pltpu.VMEM((256, WIDTH), BF16)],
        flops=0,
        nbytes=0,
    )(meta, near, across, wq, wkv, far_cols, gain)
    out_rows = jnp.concatenate([w_out, after(parts, across)[:, 2].reshape(64, WIDTH)], axis=0)
    out_all = lax.all_gather(out_rows, ROW, axis=0, tiled=True)

    partner = swap_half(kv)
    sums, maxes, dens, slots = call(
        own_kernel,
        [((ROWS, 128), F32)] * 3 + [((8, TOK), I32)],
        [VMEM] * 4,
        scratch=[pltpu.VMEM((ROWS, 128), BF16)] * 2,
        flops=4000000000,
        nbytes=3000000,
    )(q, kv, start, ids)
    pick, other_pick, chosen = call(
        route_kernel,
        [((8 * CAP, TOK), BF16)] * 2 + [((8 * CAP, WIDTH), BF16)],
        [SMEM] + [VMEM] * 2,
        flops=2000000000,
        nbytes=5000000,
    )(meta, after(near, kv), across)

    (own,) = call(order_kernel, [((2304, 512), BF16)], [VMEM] * 3, nbytes=5000000)(
        *(after(w, kv) for w in (w_gate, w_up, w_down))
    )
    pair = in_pair(piece, beside, zr)
    four = in_pair(pair, swap_near(after(pair, kv), 1), zp)
    partner, sums, pick, own, four, out_all = lax.optimization_barrier(
        (partner, sums, pick, own, four, out_all)
    )
    onward = jnp.where(zh == 0, partner, kv)
    shifted = next_group(onward)
    given_a = give_half(own, True)
    other = lax.all_gather(four, "y", axis=0, tiled=True)
    (pages,) = call(
        page_kernel,
        [((ROWS, 128), BF16)],
        [SMEM, SMEM] + [VMEM] * 2,
        scratch=[pltpu.VMEM((2 * ROWS, 128), BF16)],
        nbytes=0,
    )(meta, page_table, kv, partner)
    previous = jnp.where(zh == 0, shifted, partner)
    (heads,) = call(
        before_kernel,
        [((4, ROWS + 256, 128), BF16)],
        [VMEM] * 7,
        scratch=[pltpu.VMEM((ROWS, 128), BF16)] * 2,
        flops=0,
        nbytes=0,
    )(q, previous, start, sums, maxes, dens, pages)
    heads = lax.all_to_all(heads, "x", split_axis=0, concat_axis=0, tiled=True)
    keep, give = call(
        split_kernel,
        [((5 * TOK, 512), BF16)] * 2,
        [SMEM] + [VMEM] * 3,
        flops=0,
        nbytes=0,
    )(meta, heads, pick, other_pick)
    got = swap_core(give)
    other = after(other, give)
    given_b = give_half(other, False)
    mid, expert_out = call(
        expert_kernel,
        [((TOK, WIDTH), BF16), ((8 * CAP, WIDTH), BF16)],
        [SMEM] + [VMEM] * 6 + [HBM] * 4,
        scratch=[
            pltpu.VMEM((2, 2304, 512), BF16),
            pltpu.VMEM((2, WIDTH, 512), BF16),
            pltpu.VMEM((2, 768, 512), BF16),
            pltpu.SemaphoreType.DMA((2,)),
        ],
        flops=0,
        nbytes=0,
    )(meta, keep, got, out_all, chosen, tokens, ffn_gain[None, :], own, other, given_a, given_b)
    (cache,) = call(cache_kernel, [((TOK, 1024), BF16)], [SMEM] + [VMEM] * 2, nbytes=800000)(
        meta, after(keep, expert_out), got
    )
    returned = lax.all_to_all(
        expert_out.reshape(8, CAP, WIDTH), ROW, split_axis=0, concat_axis=0, tiled=True
    ).reshape(8 * CAP, WIDTH)
    (hidden,) = call(
        combine_kernel, [((TOK, WIDTH), BF16)], [VMEM] * 4, flops=0, nbytes=0
    )(returned, mid, slots, route_weights.T)
    return (hidden, cache.reshape(8, PAGE, 1024))


def solution(mesh):
    fine = Mesh(mesh.devices.reshape(SIZES), AXES)
    grp, tp = ("y", "zq", "zr", "zp"), ("zh", "x", "c")
    in_specs = (
        P(AXES, None),
        P(),
        P(),
        P(None, tp),
        P(None, tp),
        P(tp, None),
        P(AXES),
        P(AXES, None),
        P(AXES, None),
        P(None, tp),
        P(None, tp),
        P(tp, None),
        P(grp, None),
    )
    out_specs = (P(AXES, None), P(AXES, None, None))
    return jax.shard_map(body, mesh=fine, in_specs=in_specs, out_specs=out_specs, check_vma=False)
```

```python
import functools

import jax
import jax.numpy as jnp
import numpy as np
from jax import lax
from jax.experimental import pallas as pl
from jax.experimental.pallas import tpu as pltpu
from jax.sharding import Mesh
from jax.sharding import PartitionSpec as P

AXES = ("y", "zq", "zr", "zp", "zh", "x", "c")
SIZES = (4, 2, 2, 2, 2, 4, 2)
FLAT = (4, 8, 2, 4, 2)
ROW = ("x", "c")
PAGE = 16
CAP = 48
TOK = 128
WIDTH = 1536
ROWS = 8 * TOK
BF16 = jnp.bfloat16
F32 = jnp.float32
I32 = jnp.int32
VMEM = pl.BlockSpec(memory_space=pltpu.VMEM)
HBM = pl.BlockSpec(memory_space=pltpu.HBM)
SMEM = pl.BlockSpec(memory_space=pltpu.SMEM)
MIB = 1 << 20


def permute(block, target):
    route = []
    for source in range(int(np.prod(FLAT))):
        goal = target(*(int(v) for v in np.unravel_index(source, FLAT)))
        if goal is not None:
            route.append((source, int(np.ravel_multi_index(goal, FLAT))))
    return lax.ppermute(block, AXES, route)


def swap_core(block):
    return permute(block, lambda y, zl, zh, x, c: (y, zl, zh, x, 1 - c))


def swap_half(block):
    return permute(block, lambda y, zl, zh, x, c: (y, zl, 1 - zh, x, c))


def swap_near(block, step):
    return permute(block, lambda y, zl, zh, x, c: (y, zl ^ step, zh, x, c))


def in_pair(mine, theirs, place):
    first = jnp.where(place == 0, mine, theirs)
    return jnp.concatenate([first, jnp.where(place == 0, theirs, mine)], axis=0)


def next_group(block):
    def target(y, zl, zh, x, c):
        if zl < 7:
            return (y, zl + 1, 0, x, c) if zh == 0 else None
        return (y + 1, 0, 0, x, c) if zh == 1 and y < 3 else None

    return permute(block, target)


def give_half(block, near):
    def target(y, zl, zh, x, c):
        return (y, zl, zh, x, 1 - c) if (c == zh) != near else None

    return permute(block, target)


def gather(block, axis):
    wide = jnp.broadcast_to(block[None], (lax.axis_size(axis),) + block.shape)
    return lax.all_to_all(wide, axis, split_axis=0, concat_axis=0, tiled=True)


def after(value, *earlier):
    return lax.optimization_barrier((value,) + earlier)[0]


def call(kernel, outs, in_specs, scratch=(), flops=0, nbytes=0, limit=48):
    outs = [jax.ShapeDtypeStruct(shape, kind) for shape, kind in outs]
    return pl.pallas_call(
        kernel,
        out_shape=outs,
        in_specs=in_specs,
        out_specs=[VMEM] * len(outs),
        scratch_shapes=list(scratch),
        compiler_params=pltpu.CompilerParams(vmem_limit_bytes=limit * MIB),
        cost_estimate=pl.CostEstimate(flops=flops, bytes_accessed=nbytes, transcendentals=0),
    )


def dot_nt(left, right):
    return lax.dot_general(left, right, (((1,), (1,)), ((), ())), preferred_element_type=F32)


def dot_tn(left, right):
    return lax.dot_general(left, right, (((0,), (0,)), ((), ())), preferred_element_type=F32)


def column(lane_row):
    return jnp.transpose(jnp.broadcast_to(lane_row, (TOK, TOK)))


def rms(values, gain):
    inverse = lax.rsqrt(jnp.mean(values * values, axis=-1, keepdims=True) + 1e-05)
    return (values * inverse * gain).astype(BF16)


def pack_kernel(meta, tokens, seg, ids, out):
    own = meta[5] * TOK + lax.broadcasted_iota(I32, (1, TOK), 1)
    back = own - seg[...]
    row = lax.broadcasted_iota(I32, (16, TOK), 0)
    pieces = jnp.where(row == 0, back >> 5, jnp.where(row == 1, back & 31, 0))
    pieces = jnp.where(row == 2, ids[0:1], jnp.where(row == 3, ids[1:2], pieces))
    pieces = pieces.astype(F32).astype(BF16)
    for copy in range(4):
        out[copy, :TOK] = tokens[...]
        out[copy, TOK:, :TOK] = pieces
        out[copy, TOK:, TOK:] = jnp.zeros((16, WIDTH - TOK), BF16)


def piece_kernel(meta, wq, wkv, wo, gate, up, down, out, sems):
    y = meta[0]
    place = lax.rem(meta[1], 4)
    piece = y * 4 + lax.rem(place, 2) * 2 + place // 2
    small = pl.ds(pl.multiple_of(y * 16, 16), 16)
    deep = pl.ds(pl.multiple_of(piece * 16, 16), 16)
    pairs = [
        (wq.at[small], out.at[0:16]),
        (wkv.at[small], out.at[16:32]),
        (wo.at[small], out.at[32:48]),
    ]
    for i in range(2):
        wide = pl.ds(pl.multiple_of(piece * 96 + 48 * i, 16), 48)
        pairs.append((gate.at[wide], out.at[48:96, 512 * i : 512 * i + 256]))
        pairs.append((up.at[wide], out.at[48:96, 512 * i + 256 : 512 * i + 512]))
    for i in range(3):
        chunk = slice(512 * i, 512 * i + 512)
        pairs.append((down.at[deep, chunk], out.at[48 + 16 * i : 64 + 16 * i, 1024:]))
    copies = [pltpu.make_async_copy(a, b, sems.at[n]) for n, (a, b) in enumerate(pairs)]
    for copy in copies:
        copy.start()
    for copy in copies:
        copy.wait()


def order_kernel(gate, up, down, out):
    for e in range(16):
        rows = slice(48 * e, 48 * e + 48)
        for i in range(2):
            low = 96 * e + 48 * i
            out[rows, 512 * i : 512 * i + 256] = gate[low : low + 48]
            out[rows, 512 * i + 256 : 512 * i + 512] = up[low : low + 48]
        for i in range(3):
            low = 48 * e + 16 * i
            out[low : low + 16, 1024:] = down[16 * e : 16 * e + 16, 512 * i : 512 * i + 512]


def project_kernel(meta, near, across, wq, wkv, wo, parts, gain,
                   q_out, kv_out, start_out, wo_out, cols):
    zh, c = meta[2], meta[4]
    cols[0:64] = wq[...]
    cols[pl.ds(pl.multiple_of(128 + zh * 64, 64), 64), :] = wkv[...]
    wo_out[0:64] = wo[...]
    for i in range(4):
        cols[64 + 16 * i : 80 + 16 * i] = parts[i, 0:16]
        cols[pl.ds(pl.multiple_of(192 - zh * 64 + 16 * i, 16), 16), :] = parts[i, 16:32]
        wo_out[64 + 16 * i : 80 + 16 * i] = parts[i, 32:48]
    for k in range(4):
        for block, core in ((near, c), (across, 1 - c)):
            low = pl.multiple_of((2 * k + core) * TOK, TOK)
            normed = rms(block[k, :TOK].astype(F32), gain[...])
            result = dot_nt(normed, cols[...]).astype(BF16)
            q_out[pl.ds(low, TOK), :] = result[:, :128]
            kv_out[pl.ds(low, TOK), :] = result[:, 128:]
            pieces = block[k, TOK:, :TOK].astype(F32)
            back = column(pieces[0:1] * 32.0 + pieces[1:2])
            own = (low + lax.broadcasted_iota(I32, (TOK, TOK), 0)).astype(F32)
            start_out[pl.ds(low, TOK), :] = own - back


def route_kernel(meta, near, across, pick_out, other_out, rows_out):
    x, c = meta[3], meta[4]
    before = lax.broadcasted_iota(I32, (TOK, TOK), 0) < lax.broadcasted_iota(I32, (TOK, TOK), 1)
    before = before.astype(F32).astype(BF16)
    row = lax.broadcasted_iota(I32, (CAP, TOK), 0).astype(F32)
    for expert, out in ((x + 4 * c, pick_out), (x + 4 * (1 - c), other_out)):
        number = expert.astype(F32)
        for k in range(4):
            for block, core in ((near, c), (across, 1 - c)):
                low = pl.multiple_of((2 * k + core) * CAP, 16)
                pieces = block[k, TOK:, :TOK].astype(F32)
                named = (pieces == number).astype(F32)
                named = named[2:3] + named[3:4]
                rank = jnp.dot(
                    jnp.broadcast_to(named, (8, TOK)).astype(BF16),
                    before,
                    preferred_element_type=F32,
                )[0:1]
                pick = jnp.where((row == rank) & (named > 0.0), 1.0, 0.0).astype(BF16)
                out[pl.ds(low, CAP), :] = pick
                if out is pick_out:
                    chosen = jnp.dot(pick, block[k, :TOK], preferred_element_type=F32)
                    rows_out[pl.ds(low, CAP), :] = chosen.astype(BF16)


def split_kv(kv):
    wide = kv[...].astype(F32)
    turned = pltpu.roll(wide, 64, 1)
    low = lax.broadcasted_iota(I32, wide.shape, 1) < 64
    return (
        jnp.where(low, wide, turned).astype(BF16),
        jnp.where(low, turned, wide).astype(BF16),
    )


STEP = 256


def own_kernel(q, kv, start, ids, sum_out, max_out, den_out, slots_out, keys, values):
    keys[...], values[...] = split_kv(kv)
    low_lane = lax.broadcasted_iota(I32, (STEP, 128), 1) < 64
    for block in range(ROWS // STEP):
        low = block * STEP
        span = low + STEP
        query = q[low:span]
        position = lax.broadcasted_iota(I32, (STEP, span), 1).astype(F32)
        own = (low + lax.broadcasted_iota(I32, (STEP, span), 0)).astype(F32)
        allowed = (position <= own) & (position >= start[low:span, 0:1])
        parts = []
        for head in range(2):
            kept = jnp.where(low_lane if head == 0 else ~low_lane, query, jnp.zeros_like(query))
            scores = jnp.where(allowed, dot_nt(kept, keys[:span]) * 0.125, -1e30)
            top = jnp.max(scores, axis=-1, keepdims=True)
            weights = jnp.exp(scores - top)
            den = jnp.sum(weights, axis=-1, keepdims=True)
            part = jnp.dot(weights.astype(BF16), values[:span], preferred_element_type=F32)
            parts.append((part, top, den))
        for out, one, two in zip((sum_out, max_out, den_out), *parts):
            out[low:span] = jnp.where(low_lane, one, two)
    choice = [ids[k : k + 1].astype(F32) for k in range(2)]
    down = [column(v) for v in choice]
    earlier = lax.broadcasted_iota(I32, (TOK, TOK), 0) < lax.broadcasted_iota(I32, (TOK, TOK), 1)
    result = []
    for k in range(2):
        same = sum((down[j] == choice[k]).astype(F32) for j in range(2))
        rank = jnp.sum(jnp.where(earlier, same, 0.0), axis=0, keepdims=True).astype(I32)
        expert = ids[k : k + 1]
        result.append(((expert & 3) * 2 + (expert >> 2)) * CAP + rank)
    row = lax.broadcasted_iota(I32, (8, TOK), 0)
    slots_out[...] = jnp.where(row == 0, result[0], result[1])


def before_kernel(q, kv, start, sums, maxes, dens, pages, out, keys, values):
    keys[...], values[...] = split_kv(kv)
    low_lane = lax.broadcasted_iota(I32, (STEP, 128), 1) < 64
    for block in range(ROWS // STEP):
        low = block * STEP
        high = low + STEP
        span = ROWS - low
        query = q[low:high]
        position = (low - ROWS + lax.broadcasted_iota(I32, (STEP, span), 1)).astype(F32)
        allowed = position >= start[low:high, 0:1]
        parts = []
        for head in range(2):
            kept = jnp.where(low_lane if head == 0 else ~low_lane, query, jnp.zeros_like(query))
            scores = jnp.where(allowed, dot_nt(kept, keys[low:]) * 0.125, -1e30)
            first = maxes[low:high, head * 64 : head * 64 + 1]
            top = jnp.maximum(first, jnp.max(scores, axis=-1, keepdims=True))
            weights = jnp.exp(scores - top)
            scale = jnp.exp(first - top)
            den = jnp.sum(weights, axis=-1, keepdims=True)
            part = jnp.dot(weights.astype(BF16), values[low:], preferred_element_type=F32)
            parts.append((part, scale, den))
        part, scale, den = (jnp.where(low_lane, one, two) for one, two in zip(*parts))
        total = sums[low:high] * scale + part
        result = (total / (dens[low:high] * scale + den)).astype(BF16)
        for copy in range(4):
            out[copy, low:high, :] = result
    for k in range(4):
        out[k, ROWS:, :] = pages[k * 256 : k * 256 + 256]


def page_kernel(meta, table, kv, partner, out, group):
    zh = meta[2]
    group[pl.ds(pl.multiple_of(zh * ROWS, ROWS), ROWS), :] = kv[...]
    group[pl.ds(pl.multiple_of((1 - zh) * ROWS, ROWS), ROWS), :] = partner[...]

    def place(block, carry):
        page = table[0, block] - zh * 64

        @pl.when((page >= 0) & (page < 64))
        def _():
            out[pl.ds(pl.multiple_of(page * PAGE, PAGE), PAGE), :] = group[
                pl.ds(pl.multiple_of(block * PAGE, PAGE), PAGE), :
            ]

        return carry

    lax.fori_loop(0, 128, place, 0)


def cache_kernel(meta, keep, got, out):
    c = meta[4]
    low = lax.broadcasted_iota(I32, (TOK, 128), 1) < 64
    for pair in range(4):
        lanes = slice(pair * 128, pair * 128 + 128)
        mine = keep[4 * TOK :, lanes].astype(F32)
        theirs = got[4 * TOK :, lanes].astype(F32)
        one = jnp.where(c == 0, mine, theirs)
        two = jnp.where(c == 0, theirs, mine)
        out[:, lanes] = jnp.where(low, one, pltpu.roll(two, 64, 1)).astype(BF16)
        lanes = slice(512 + pair * 128, 640 + pair * 128)
        out[:, lanes] = jnp.where(low, pltpu.roll(one, 64, 1), two).astype(BF16)


def choose(slots, k):
    place = lax.broadcasted_iota(I32, (8 * CAP, TOK), 0)
    return place == slots[k : k + 1]


def split_kernel(meta, heads, pick, other, keep_out, give_out):
    x, c = meta[3], meta[4]
    for d in range(8):
        rows = jnp.concatenate([heads[k, d * TOK : d * TOK + TOK] for k in range(4)], axis=1)
        low = slice(d * CAP, d * CAP + CAP)
        keep_out[low] = jnp.dot(pick[low], rows, preferred_element_type=F32).astype(BF16)
        give_out[low] = jnp.dot(other[low], rows, preferred_element_type=F32).astype(BF16)
    for out, core in ((keep_out, c), (give_out, 1 - c)):
        low = pl.multiple_of((2 * x + core) * TOK, TOK)
        page = pl.multiple_of(ROWS + core * TOK, TOK)
        for k in range(4):
            lanes = slice(k * 128, k * 128 + 128)
            out[8 * CAP : 4 * TOK, lanes] = heads[k, pl.ds(low, TOK), :]
            out[4 * TOK :, lanes] = heads[k, pl.ds(page, TOK), :]


def expert_kernel(meta, keep, got, wo_all, rows, tokens, gain, own, other, given_a, given_b,
                  mid_out, out, raw, wide, deep, sems):
    zh, c = meta[2], meta[4]

    @pl.when(c == zh)
    def _():
        pltpu.make_async_copy(own, raw.at[0], sems.at[0]).start()
        pltpu.make_async_copy(given_a, raw.at[1], sems.at[1]).start()

    @pl.when(c != zh)
    def _():
        pltpu.make_async_copy(other, raw.at[0], sems.at[0]).start()
        pltpu.make_async_copy(given_b, raw.at[1], sems.at[1]).start()

    tiles = []
    for k in range(4):
        one = keep[: 4 * TOK, k * 128 : k * 128 + 128]
        two = got[: 4 * TOK, k * 128 : k * 128 + 128]
        tiles += [jnp.where(c == 0, one, two), jnp.where(c == 0, two, one)]
    total = jnp.dot(jnp.concatenate(tiles, axis=1), wo_all[...], preferred_element_type=F32)
    mid_out[...] = (tokens[...].astype(F32) + total[8 * CAP :]).astype(BF16)
    mid = (rows[...].astype(F32) + total[: 8 * CAP]).astype(BF16)
    arrived = rms(mid.astype(F32), gain[...])
    acts = []
    for half, source in enumerate((own, given_a)):
        pltpu.make_async_copy(source, raw.at[half], sems.at[half]).wait()
        for e in range(16):
            for i in range(2):
                low = 96 * e + 48 * i
                wide[half, low : low + 48] = raw[
                    half, 48 * e : 48 * e + 48, 512 * i : 512 * i + 512
                ]
            for i in range(3):
                low = 48 * e + 16 * i
                deep[half, i * 256 + e * 16 : i * 256 + e * 16 + 16] = raw[
                    half, low : low + 16, 1024:
                ]
        both = jnp.dot(arrived, wide[half], preferred_element_type=F32)
        gate, up = both[:, :256], both[:, 256:]
        acts.append((gate / (1.0 + jnp.exp(-gate)) * up).astype(BF16))
    for i in range(3):
        chunk = slice(i * 256, i * 256 + 256)
        total = jnp.dot(acts[0], deep[0, chunk], preferred_element_type=F32)
        total += jnp.dot(acts[1], deep[1, chunk], preferred_element_type=F32)
        out[:, i * 512 : i * 512 + 512] = total.astype(BF16)


def combine_kernel(returned, mid, slots, weights, out):
    total = mid[...].astype(F32)
    for k in range(2):
        pick = choose(slots, k).astype(F32).astype(BF16)
        chosen = dot_tn(pick, returned[...])
        total += chosen * column(weights[k : k + 1])[:, 0:1]
    out[...] = total.astype(BF16)


def body(
    tokens,
    attn_gain,
    ffn_gain,
    w_query,
    key_value_weight,
    w_out,
    segment_ids,
    expert_ids,
    route_weights,
    w_gate,
    w_up,
    w_down,
    page_table,
):
    y, zq, zr, zp, zh, x, c = (lax.axis_index(name) for name in AXES)
    zl = zq * 4 + zr * 2 + zp
    place = (((y * 8 + zl) * 2 + zh) * 4 + x) * 2 + c
    meta = jnp.stack([y, zl, zh, x, c, place]).astype(I32)
    wq, wkv = w_query.T, key_value_weight.T
    ids = expert_ids.T

    (block,) = call(
        pack_kernel, [((4, TOK + 16, WIDTH), BF16)], [SMEM] + [VMEM] * 3, nbytes=0
    )(meta, tokens, segment_ids[None, :], ids)
    (piece,) = call(
        piece_kernel,
        [((96, WIDTH), BF16)],
        [SMEM] + [HBM] * 6,
        scratch=[pltpu.SemaphoreType.DMA((10,))],
    )(meta, wq, wkv, w_out, w_gate, w_up, w_down)
    near = lax.all_to_all(block, "x", split_axis=0, concat_axis=0, tiled=True)
    near, piece = lax.optimization_barrier((near, swap_half(piece)))
    parts = gather(piece[:48], "y")
    across = swap_core(near)
    q, kv, start, out_rows = call(
        project_kernel,
        [((ROWS, 128), BF16), ((ROWS, 128), BF16), ((ROWS, 128), F32), ((128, WIDTH), BF16)],
        [SMEM] + [VMEM] * 7,
        scratch=[pltpu.VMEM((256, WIDTH), BF16)],
    )(meta, near, across, wq, wkv, w_out, parts, attn_gain[None, :])
    out_all = lax.all_gather(out_rows, ROW, axis=0, tiled=True)

    partner = swap_half(kv)
    sums, maxes, dens, slots = call(
        own_kernel,
        [((ROWS, 128), F32)] * 3 + [((8, TOK), I32)],
        [VMEM] * 4,
        scratch=[pltpu.VMEM((ROWS, 128), BF16)] * 2,
        flops=4000000000,
        nbytes=3000000,
    )(q, kv, start, ids)
    pick, other_pick, chosen = call(
        route_kernel,
        [((8 * CAP, TOK), BF16)] * 2 + [((8 * CAP, WIDTH), BF16)],
        [SMEM] + [VMEM] * 2,
        flops=2000000000,
        nbytes=5000000,
    )(meta, after(near, kv), across)

    (own,) = call(order_kernel, [((768, WIDTH), BF16)], [VMEM] * 3, nbytes=5000000)(
        *(after(w, kv) for w in (w_gate, w_up, w_down))
    )
    piece = after(piece[48:], kv)
    pair = in_pair(piece, swap_near(piece, 2), zr)
    four = in_pair(pair, swap_near(pair, 1), zp)
    partner, sums, pick, own, four, out_all = lax.optimization_barrier(
        (partner, sums, pick, own, four, out_all)
    )
    onward = jnp.where(zh == 0, partner, kv)
    shifted = next_group(onward)
    given_a = give_half(own, True)
    other = lax.all_gather(four, "y", axis=0, tiled=True)
    (pages,) = call(
        page_kernel,
        [((ROWS, 128), BF16)],
        [SMEM, SMEM] + [VMEM] * 2,
        scratch=[pltpu.VMEM((2 * ROWS, 128), BF16)],
        nbytes=0,
    )(meta, page_table, kv, partner)
    previous = jnp.where(zh == 0, shifted, partner)
    (heads,) = call(
        before_kernel,
        [((4, ROWS + 256, 128), BF16)],
        [VMEM] * 7,
        scratch=[pltpu.VMEM((ROWS, 128), BF16)] * 2,
        flops=0,
        nbytes=0,
    )(q, previous, start, sums, maxes, dens, pages)
    heads = lax.all_to_all(heads, "x", split_axis=0, concat_axis=0, tiled=True)
    keep, give = call(
        split_kernel,
        [((5 * TOK, 512), BF16)] * 2,
        [SMEM] + [VMEM] * 3,
        flops=0,
        nbytes=0,
    )(meta, heads, pick, other_pick)
    got = swap_core(give)
    other = after(other, give)
    given_b = give_half(other, False)
    mid, expert_out = call(
        expert_kernel,
        [((TOK, WIDTH), BF16), ((8 * CAP, WIDTH), BF16)],
        [SMEM] + [VMEM] * 6 + [HBM] * 4,
        scratch=[
            pltpu.VMEM((2, 768, WIDTH), BF16),
            pltpu.VMEM((2, WIDTH, 512), BF16),
            pltpu.VMEM((2, 768, 512), BF16),
            pltpu.SemaphoreType.DMA((2,)),
        ],
        flops=0,
        nbytes=0,
    )(meta, keep, got, out_all, chosen, tokens, ffn_gain[None, :], own, other, given_a, given_b)
    (cache,) = call(cache_kernel, [((TOK, 1024), BF16)], [SMEM] + [VMEM] * 2, nbytes=800000)(
        meta, after(keep, expert_out), got
    )
    returned = lax.all_to_all(
        expert_out.reshape(8, CAP, WIDTH), ROW, split_axis=0, concat_axis=0, tiled=True
    ).reshape(8 * CAP, WIDTH)
    (hidden,) = call(
        combine_kernel, [((TOK, WIDTH), BF16)], [VMEM] * 4, flops=0, nbytes=0
    )(returned, mid, slots, route_weights.T)
    return (hidden, cache.reshape(8, PAGE, 1024))


def solution(mesh):
    fine = Mesh(mesh.devices.reshape(SIZES), AXES)
    grp, tp = ("y", "zq", "zr", "zp"), ("zh", "x", "c")
    in_specs = (
        P(AXES, None),
        P(),
        P(),
        P(None, tp),
        P(None, tp),
        P(tp, None),
        P(AXES),
        P(AXES, None),
        P(AXES, None),
        P(None, tp),
        P(None, tp),
        P(tp, None),
        P(grp, None),
    )
    out_specs = (P(AXES, None), P(AXES, None, None))
    return jax.shard_map(body, mesh=fine, in_specs=in_specs, out_specs=out_specs, check_vma=False)
```

```python
import functools

import jax
import jax.numpy as jnp
import numpy as np
from jax import lax
from jax.experimental import pallas as pl
from jax.experimental.pallas import tpu as pltpu
from jax.sharding import Mesh
from jax.sharding import PartitionSpec as P

AXES = ("y", "zq", "zr", "zp", "zh", "x", "c")
SIZES = (4, 2, 2, 2, 2, 4, 2)
FLAT = (4, 8, 2, 4, 2)
ROW = ("x", "c")
PAGE = 16
CAP = 48
TOK = 128
WIDTH = 1536
ROWS = 8 * TOK
BF16 = jnp.bfloat16
F32 = jnp.float32
I32 = jnp.int32
VMEM = pl.BlockSpec(memory_space=pltpu.VMEM)
HBM = pl.BlockSpec(memory_space=pltpu.HBM)
SMEM = pl.BlockSpec(memory_space=pltpu.SMEM)
MIB = 1 << 20


def permute(block, target):
    route = []
    for source in range(int(np.prod(FLAT))):
        goal = target(*(int(v) for v in np.unravel_index(source, FLAT)))
        if goal is not None:
            route.append((source, int(np.ravel_multi_index(goal, FLAT))))
    return lax.ppermute(block, AXES, route)


def swap_core(block):
    return permute(block, lambda y, zl, zh, x, c: (y, zl, zh, x, 1 - c))


def swap_half(block):
    return permute(block, lambda y, zl, zh, x, c: (y, zl, 1 - zh, x, c))


def swap_near(block, step):
    return permute(block, lambda y, zl, zh, x, c: (y, zl ^ step, zh, x, c))


def in_pair(mine, theirs, place):
    first = jnp.where(place == 0, mine, theirs)
    return jnp.concatenate([first, jnp.where(place == 0, theirs, mine)], axis=0)


def next_group(block):
    def target(y, zl, zh, x, c):
        if zl < 7:
            return (y, zl + 1, 0, x, c) if zh == 0 else None
        return (y + 1, 0, 0, x, c) if zh == 1 and y < 3 else None

    return permute(block, target)


def give_half(block, near):
    def target(y, zl, zh, x, c):
        return (y, zl, zh, x, 1 - c) if (c == zh) != near else None

    return permute(block, target)


def gather(block, axis):
    wide = jnp.broadcast_to(block[None], (lax.axis_size(axis),) + block.shape)
    return lax.all_to_all(wide, axis, split_axis=0, concat_axis=0, tiled=True)


def after(value, *earlier):
    return lax.optimization_barrier((value,) + earlier)[0]


def call(kernel, outs, in_specs, scratch=(), flops=0, nbytes=0, limit=16):
    outs = [jax.ShapeDtypeStruct(shape, kind) for shape, kind in outs]
    return pl.pallas_call(
        kernel,
        out_shape=outs,
        in_specs=in_specs,
        out_specs=[VMEM] * len(outs),
        scratch_shapes=list(scratch),
        compiler_params=pltpu.CompilerParams(vmem_limit_bytes=limit * MIB),
        cost_estimate=pl.CostEstimate(flops=flops, bytes_accessed=nbytes, transcendentals=0),
    )


def dot_nt(left, right):
    return lax.dot_general(left, right, (((1,), (1,)), ((), ())), preferred_element_type=F32)


def dot_tn(left, right):
    return lax.dot_general(left, right, (((0,), (0,)), ((), ())), preferred_element_type=F32)


def column(lane_row):
    return jnp.transpose(jnp.broadcast_to(lane_row, (TOK, TOK)))


def rms(values, gain):
    inverse = lax.rsqrt(jnp.mean(values * values, axis=-1, keepdims=True) + 1e-05)
    return (values * inverse * gain).astype(BF16)


def pack_kernel(meta, tokens, seg, ids, out):
    own = meta[5] * TOK + lax.broadcasted_iota(I32, (1, TOK), 1)
    back = own - seg[...]
    row = lax.broadcasted_iota(I32, (16, TOK), 0)
    pieces = jnp.where(row == 0, back >> 5, jnp.where(row == 1, back & 31, 0))
    pieces = jnp.where(row == 2, ids[0:1], jnp.where(row == 3, ids[1:2], pieces))
    pieces = pieces.astype(F32).astype(BF16)
    for copy in range(4):
        out[copy, :TOK] = tokens[...]
        out[copy, TOK:, :TOK] = pieces
        out[copy, TOK:, TOK:] = jnp.zeros((16, WIDTH - TOK), BF16)


def piece_kernel(meta, wq, wkv, wo, gate, up, down, out, sems):
    y = meta[0]
    place = lax.rem(meta[1], 4)
    piece = y * 4 + lax.rem(place, 2) * 2 + place // 2
    small = pl.ds(pl.multiple_of(y * 16, 16), 16)
    deep = pl.ds(pl.multiple_of(piece * 16, 16), 16)
    pairs = [
        (wq.at[small], out.at[0:16]),
        (wkv.at[small], out.at[16:32]),
        (wo.at[small], out.at[32:48]),
    ]
    for i in range(2):
        wide = pl.ds(pl.multiple_of(piece * 96 + 48 * i, 16), 48)
        pairs.append((gate.at[wide], out.at[48:96, 512 * i : 512 * i + 256]))
        pairs.append((up.at[wide], out.at[48:96, 512 * i + 256 : 512 * i + 512]))
    for i in range(3):
        chunk = slice(512 * i, 512 * i + 512)
        pairs.append((down.at[deep, chunk], out.at[48 + 16 * i : 64 + 16 * i, 1024:]))
    copies = [pltpu.make_async_copy(a, b, sems.at[n]) for n, (a, b) in enumerate(pairs)]
    for copy in copies:
        copy.start()
    for copy in copies:
        copy.wait()


def order_kernel(gate, up, down, out):
    for e in range(16):
        rows = slice(48 * e, 48 * e + 48)
        for i in range(2):
            low = 96 * e + 48 * i
            out[rows, 512 * i : 512 * i + 256] = gate[low : low + 48]
            out[rows, 512 * i + 256 : 512 * i + 512] = up[low : low + 48]
        for i in range(3):
            low = 48 * e + 16 * i
            out[low : low + 16, 1024:] = down[16 * e : 16 * e + 16, 512 * i : 512 * i + 512]


def project_kernel(meta, near, across, wq, wkv, wo, parts, gain,
                   q_out, kv_out, start_out, wo_out, cols):
    zh, c = meta[2], meta[4]
    cols[0:64] = wq[...]
    cols[pl.ds(pl.multiple_of(128 + zh * 64, 64), 64), :] = wkv[...]
    wo_out[0:64] = wo[...]
    for i in range(4):
        cols[64 + 16 * i : 80 + 16 * i] = parts[i, 0:16]
        cols[pl.ds(pl.multiple_of(192 - zh * 64 + 16 * i, 16), 16), :] = parts[i, 16:32]
        wo_out[64 + 16 * i : 80 + 16 * i] = parts[i, 32:48]
    for k in range(4):
        for block, core in ((near, c), (across, 1 - c)):
            low = pl.multiple_of((2 * k + core) * TOK, TOK)
            normed = rms(block[k, :TOK].astype(F32), gain[...])
            result = dot_nt(normed, cols[...]).astype(BF16)
            q_out[pl.ds(low, TOK), :] = result[:, :128]
            kv_out[pl.ds(low, TOK), :] = result[:, 128:]
            pieces = block[k, TOK:, :TOK].astype(F32)
            back = column(pieces[0:1] * 32.0 + pieces[1:2])
            own = (low + lax.broadcasted_iota(I32, (TOK, TOK), 0)).astype(F32)
            start_out[pl.ds(low, TOK), :] = own - back


def route_kernel(meta, near, across, pick_out, other_out, rows_out):
    x, c = meta[3], meta[4]
    before = lax.broadcasted_iota(I32, (TOK, TOK), 0) < lax.broadcasted_iota(I32, (TOK, TOK), 1)
    before = before.astype(F32).astype(BF16)
    row = lax.broadcasted_iota(I32, (CAP, TOK), 0).astype(F32)
    for expert, out in ((x + 4 * c, pick_out), (x + 4 * (1 - c), other_out)):
        number = expert.astype(F32)
        for k in range(4):
            for block, core in ((near, c), (across, 1 - c)):
                low = pl.multiple_of((2 * k + core) * CAP, 16)
                pieces = block[k, TOK:, :TOK].astype(F32)
                named = (pieces == number).astype(F32)
                named = named[2:3] + named[3:4]
                rank = jnp.dot(
                    jnp.broadcast_to(named, (8, TOK)).astype(BF16),
                    before,
                    preferred_element_type=F32,
                )[0:1]
                pick = jnp.where((row == rank) & (named > 0.0), 1.0, 0.0).astype(BF16)
                out[pl.ds(low, CAP), :] = pick
                if out is pick_out:
                    chosen = jnp.dot(pick, block[k, :TOK], preferred_element_type=F32)
                    rows_out[pl.ds(low, CAP), :] = chosen.astype(BF16)


def split_kv(kv):
    wide = kv[...].astype(F32)
    turned = pltpu.roll(wide, 64, 1)
    low = lax.broadcasted_iota(I32, wide.shape, 1) < 64
    return (
        jnp.where(low, wide, turned).astype(BF16),
        jnp.where(low, turned, wide).astype(BF16),
    )


STEP = 256


def own_kernel(q, kv, start, ids, sum_out, stat_out, slots_out, keys, values):
    keys[...], values[...] = split_kv(kv)
    low_lane = lax.broadcasted_iota(I32, (STEP, 128), 1) < 64
    for block in range(ROWS // STEP):
        low = block * STEP
        span = low + STEP
        query = q[low:span]
        position = lax.broadcasted_iota(I32, (STEP, span), 1).astype(F32)
        own = (low + lax.broadcasted_iota(I32, (STEP, span), 0)).astype(F32)
        allowed = (position <= own) & (position >= start[low:span, 0:1])
        parts = []
        for head in range(2):
            kept = jnp.where(low_lane if head == 0 else ~low_lane, query, jnp.zeros_like(query))
            scores = jnp.where(allowed, dot_nt(kept, keys[:span]) * 0.125, -1e30)
            top = jnp.max(scores, axis=-1, keepdims=True)
            weights = jnp.exp(scores - top)
            den = jnp.sum(weights, axis=-1, keepdims=True)
            part = jnp.dot(weights.astype(BF16), values[:span], preferred_element_type=F32)
            parts.append((part, top, den))
        sum_out[low:span] = jnp.where(low_lane, parts[0][0], parts[1][0])
        lane = lax.broadcasted_iota(I32, (STEP, 128), 1)
        stats = jnp.where(lane == 0, start[low:span, 0:1], parts[0][1])
        for n, column_of in ((2, parts[1][1]), (3, parts[0][2]), (4, parts[1][2])):
            stats = jnp.where(lane == n, column_of, stats)
        stat_out[low:span] = stats
    choice = [ids[k : k + 1].astype(F32) for k in range(2)]
    down = [column(v) for v in choice]
    earlier = lax.broadcasted_iota(I32, (TOK, TOK), 0) < lax.broadcasted_iota(I32, (TOK, TOK), 1)
    result = []
    for k in range(2):
        same = sum((down[j] == choice[k]).astype(F32) for j in range(2))
        rank = jnp.sum(jnp.where(earlier, same, 0.0), axis=0, keepdims=True).astype(I32)
        expert = ids[k : k + 1]
        result.append(((expert & 3) * 2 + (expert >> 2)) * CAP + rank)
    row = lax.broadcasted_iota(I32, (8, TOK), 0)
    slots_out[...] = jnp.where(row == 0, result[0], result[1])


def before_kernel(q, kv, sums, stats, pages, out, keys, values):
    keys[...], values[...] = split_kv(kv)
    low_lane = lax.broadcasted_iota(I32, (STEP, 128), 1) < 64
    for block in range(ROWS // STEP):
        low = block * STEP
        high = low + STEP
        span = ROWS - low
        query = q[low:high]
        position = (low - ROWS + lax.broadcasted_iota(I32, (STEP, span), 1)).astype(F32)
        allowed = position >= stats[low:high, 0:1]
        parts = []
        for head in range(2):
            kept = jnp.where(low_lane if head == 0 else ~low_lane, query, jnp.zeros_like(query))
            scores = jnp.where(allowed, dot_nt(kept, keys[low:]) * 0.125, -1e30)
            first = stats[low:high, 1 + head : 2 + head]
            top = jnp.maximum(first, jnp.max(scores, axis=-1, keepdims=True))
            weights = jnp.exp(scores - top)
            scale = jnp.exp(first - top)
            den = jnp.sum(weights, axis=-1, keepdims=True)
            den += stats[low:high, 3 + head : 4 + head] * scale
            part = jnp.dot(weights.astype(BF16), values[low:], preferred_element_type=F32)
            parts.append((part, scale, den))
        part, scale, den = (jnp.where(low_lane, one, two) for one, two in zip(*parts))
        total = sums[low:high] * scale + part
        result = (total / den).astype(BF16)
        for copy in range(4):
            out[copy, low:high, :] = result
    for k in range(4):
        out[k, ROWS:, :] = pages[k * 256 : k * 256 + 256]


def page_kernel(meta, table, kv, partner, out, group):
    zh = meta[2]
    group[pl.ds(pl.multiple_of(zh * ROWS, ROWS), ROWS), :] = kv[...]
    group[pl.ds(pl.multiple_of((1 - zh) * ROWS, ROWS), ROWS), :] = partner[...]

    def place(block, carry):
        page = table[0, block] - zh * 64

        @pl.when((page >= 0) & (page < 64))
        def _():
            out[pl.ds(pl.multiple_of(page * PAGE, PAGE), PAGE), :] = group[
                pl.ds(pl.multiple_of(block * PAGE, PAGE), PAGE), :
            ]

        return carry

    lax.fori_loop(0, 128, place, 0)


def cache_kernel(meta, keep, got, out):
    c = meta[4]
    low = lax.broadcasted_iota(I32, (TOK, 128), 1) < 64
    for pair in range(4):
        lanes = slice(pair * 128, pair * 128 + 128)
        mine = keep[4 * TOK :, lanes].astype(F32)
        theirs = got[4 * TOK :, lanes].astype(F32)
        one = jnp.where(c == 0, mine, theirs)
        two = jnp.where(c == 0, theirs, mine)
        out[:, lanes] = jnp.where(low, one, pltpu.roll(two, 64, 1)).astype(BF16)
        lanes = slice(512 + pair * 128, 640 + pair * 128)
        out[:, lanes] = jnp.where(low, pltpu.roll(one, 64, 1), two).astype(BF16)


def choose(slots, k):
    place = lax.broadcasted_iota(I32, (8 * CAP, TOK), 0)
    return place == slots[k : k + 1]


def split_kernel(meta, heads, pick, other, keep_out, give_out):
    x, c = meta[3], meta[4]
    for d in range(8):
        rows = jnp.concatenate([heads[k, d * TOK : d * TOK + TOK] for k in range(4)], axis=1)
        low = slice(d * CAP, d * CAP + CAP)
        keep_out[low] = jnp.dot(pick[low], rows, preferred_element_type=F32).astype(BF16)
        give_out[low] = jnp.dot(other[low], rows, preferred_element_type=F32).astype(BF16)
    for out, core in ((keep_out, c), (give_out, 1 - c)):
        low = pl.multiple_of((2 * x + core) * TOK, TOK)
        page = pl.multiple_of(ROWS + core * TOK, TOK)
        for k in range(4):
            lanes = slice(k * 128, k * 128 + 128)
            out[8 * CAP : 4 * TOK, lanes] = heads[k, pl.ds(low, TOK), :]
            out[4 * TOK :, lanes] = heads[k, pl.ds(page, TOK), :]


def expert_kernel(meta, keep, got, wo_all, rows, tokens, gain, own, other, given_a, given_b,
                  mid_out, out, raw, wide, deep, sems):
    zh, c = meta[2], meta[4]

    @pl.when(c == zh)
    def _():
        pltpu.make_async_copy(own, raw.at[0], sems.at[0]).start()
        pltpu.make_async_copy(given_a, raw.at[1], sems.at[1]).start()

    @pl.when(c != zh)
    def _():
        pltpu.make_async_copy(other, raw.at[0], sems.at[0]).start()
        pltpu.make_async_copy(given_b, raw.at[1], sems.at[1]).start()

    tiles = []
    for k in range(4):
        one = keep[: 4 * TOK, k * 128 : k * 128 + 128]
        two = got[: 4 * TOK, k * 128 : k * 128 + 128]
        tiles += [jnp.where(c == 0, one, two), jnp.where(c == 0, two, one)]
    total = jnp.dot(jnp.concatenate(tiles, axis=1), wo_all[...], preferred_element_type=F32)
    mid_out[...] = (tokens[...].astype(F32) + total[8 * CAP :]).astype(BF16)
    mid = (rows[...].astype(F32) + total[: 8 * CAP]).astype(BF16)
    arrived = rms(mid.astype(F32), gain[...])
    acts = []
    for half, source in enumerate((own, given_a)):
        pltpu.make_async_copy(source, raw.at[half], sems.at[half]).wait()
        for e in range(16):
            for i in range(2):
                low = 96 * e + 48 * i
                wide[half, low : low + 48] = raw[
                    half, 48 * e : 48 * e + 48, 512 * i : 512 * i + 512
                ]
            for i in range(3):
                low = 48 * e + 16 * i
                deep[half, i * 256 + e * 16 : i * 256 + e * 16 + 16] = raw[
                    half, low : low + 16, 1024:
                ]
        both = jnp.dot(arrived, wide[half], preferred_element_type=F32)
        gate, up = both[:, :256], both[:, 256:]
        acts.append((gate / (1.0 + jnp.exp(-gate)) * up).astype(BF16))
    for i in range(3):
        chunk = slice(i * 256, i * 256 + 256)
        total = jnp.dot(acts[0], deep[0, chunk], preferred_element_type=F32)
        total += jnp.dot(acts[1], deep[1, chunk], preferred_element_type=F32)
        out[:, i * 512 : i * 512 + 512] = total.astype(BF16)


def combine_kernel(returned, mid, slots, weights, out):
    total = mid[...].astype(F32)
    for k in range(2):
        pick = choose(slots, k).astype(F32).astype(BF16)
        chosen = dot_tn(pick, returned[...])
        total += chosen * column(weights[k : k + 1])[:, 0:1]
    out[...] = total.astype(BF16)


def body(
    tokens,
    attn_gain,
    ffn_gain,
    w_query,
    key_value_weight,
    w_out,
    segment_ids,
    expert_ids,
    route_weights,
    w_gate,
    w_up,
    w_down,
    page_table,
):
    y, zq, zr, zp, zh, x, c = (lax.axis_index(name) for name in AXES)
    zl = zq * 4 + zr * 2 + zp
    place = (((y * 8 + zl) * 2 + zh) * 4 + x) * 2 + c
    meta = jnp.stack([y, zl, zh, x, c, place]).astype(I32)
    wq, wkv = w_query.T, key_value_weight.T
    ids = expert_ids.T

    (block,) = call(
        pack_kernel, [((4, TOK + 16, WIDTH), BF16)], [SMEM] + [VMEM] * 3, nbytes=0
    )(meta, tokens, segment_ids[None, :], ids)
    (piece,) = call(
        piece_kernel,
        [((96, WIDTH), BF16)],
        [SMEM] + [HBM] * 6,
        scratch=[pltpu.SemaphoreType.DMA((10,))],
    )(meta, wq, wkv, w_out, w_gate, w_up, w_down)
    near = lax.all_to_all(block, "x", split_axis=0, concat_axis=0, tiled=True)
    near, piece = lax.optimization_barrier((near, swap_half(piece)))
    parts = gather(piece[:48], "y")
    across = swap_core(near)
    beside = swap_near(piece[48:], 2)
    gain, beside = lax.optimization_barrier((attn_gain[None, :], beside))
    q, kv, start, out_rows = call(
        project_kernel,
        [((ROWS, 128), BF16), ((ROWS, 128), BF16), ((ROWS, 128), F32), ((128, WIDTH), BF16)],
        [SMEM] + [VMEM] * 7,
        scratch=[pltpu.VMEM((256, WIDTH), BF16)],
    )(meta, near, across, wq, wkv, w_out, parts, gain)
    out_all = lax.all_gather(out_rows, ROW, axis=0, tiled=True)

    partner = swap_half(kv)
    sums, stats, slots = call(
        own_kernel,
        [((ROWS, 128), F32)] * 2 + [((8, TOK), I32)],
        [VMEM] * 4,
        scratch=[pltpu.VMEM((ROWS, 128), BF16)] * 2,
        flops=4000000000,
        nbytes=3000000,
    )(q, kv, start, ids)
    pick, other_pick, chosen = call(
        route_kernel,
        [((8 * CAP, TOK), BF16)] * 2 + [((8 * CAP, WIDTH), BF16)],
        [SMEM] + [VMEM] * 2,
        flops=2000000000,
        nbytes=5000000,
    )(meta, after(near, kv), across)

    (own,) = call(order_kernel, [((768, WIDTH), BF16)], [VMEM] * 3, nbytes=5000000)(
        *(after(w, kv) for w in (w_gate, w_up, w_down))
    )
    pair = in_pair(after(piece[48:], kv), after(beside, kv), zr)
    four = in_pair(pair, swap_near(pair, 1), zp)
    partner, sums, pick, own, four, out_all = lax.optimization_barrier(
        (partner, sums, pick, own, four, out_all)
    )
    onward = jnp.where(zh == 0, partner, kv)
    shifted = next_group(onward)
    given_a = give_half(own, True)
    other = lax.all_gather(four, "y", axis=0, tiled=True)
    (pages,) = call(
        page_kernel,
        [((ROWS, 128), BF16)],
        [SMEM, SMEM] + [VMEM] * 2,
        scratch=[pltpu.VMEM((2 * ROWS, 128), BF16)],
        nbytes=0,
    )(meta, page_table, kv, partner)
    previous = jnp.where(zh == 0, shifted, partner)
    (heads,) = call(
        before_kernel,
        [((4, ROWS + 256, 128), BF16)],
        [VMEM] * 5,
        scratch=[pltpu.VMEM((ROWS, 128), BF16)] * 2,
        flops=0,
        nbytes=0,
    )(q, previous, sums, stats, pages)
    heads = lax.all_to_all(heads, "x", split_axis=0, concat_axis=0, tiled=True)
    keep, give = call(
        split_kernel,
        [((5 * TOK, 512), BF16)] * 2,
        [SMEM] + [VMEM] * 3,
        flops=0,
        nbytes=0,
    )(meta, heads, pick, other_pick)
    got = swap_core(give)
    other = after(other, give)
    given_b = give_half(other, False)
    mid, expert_out = call(
        expert_kernel,
        [((TOK, WIDTH), BF16), ((8 * CAP, WIDTH), BF16)],
        [SMEM] + [VMEM] * 6 + [HBM] * 4,
        scratch=[
            pltpu.VMEM((2, 768, WIDTH), BF16),
            pltpu.VMEM((2, WIDTH, 512), BF16),
            pltpu.VMEM((2, 768, 512), BF16),
            pltpu.SemaphoreType.DMA((2,)),
        ],
        limit=40,
        flops=0,
        nbytes=0,
    )(meta, keep, got, out_all, chosen, tokens, ffn_gain[None, :], own, other, given_a, given_b)
    (cache,) = call(cache_kernel, [((TOK, 1024), BF16)], [SMEM] + [VMEM] * 2, nbytes=800000)(
        meta, after(keep, expert_out), got
    )
    returned = lax.all_to_all(
        expert_out.reshape(8, CAP, WIDTH), ROW, split_axis=0, concat_axis=0, tiled=True
    ).reshape(8 * CAP, WIDTH)
    (hidden,) = call(
        combine_kernel, [((TOK, WIDTH), BF16)], [VMEM] * 4, flops=0, nbytes=0
    )(returned, mid, slots, route_weights.T)
    return (hidden, cache.reshape(8, PAGE, 1024))


def solution(mesh):
    fine = Mesh(mesh.devices.reshape(SIZES), AXES)
    grp, tp = ("y", "zq", "zr", "zp"), ("zh", "x", "c")
    in_specs = (
        P(AXES, None),
        P(),
        P(),
        P(None, tp),
        P(None, tp),
        P(tp, None),
        P(AXES),
        P(AXES, None),
        P(AXES, None),
        P(None, tp),
        P(None, tp),
        P(tp, None),
        P(grp, None),
    )
    out_specs = (P(AXES, None), P(AXES, None, None))
    return jax.shard_map(body, mesh=fine, in_specs=in_specs, out_specs=out_specs, check_vma=False)
```

```python
import functools

import jax
import jax.numpy as jnp
import numpy as np
from jax import lax
from jax.experimental import pallas as pl
from jax.experimental.pallas import tpu as pltpu
from jax.sharding import Mesh
from jax.sharding import PartitionSpec as P

AXES = ("y", "zq", "zr", "zp", "zh", "x", "c")
SIZES = (4, 2, 2, 2, 2, 4, 2)
FLAT = (4, 8, 2, 4, 2)
ROW = ("x", "c")
PAGE = 16
CAP = 48
TOK = 128
WIDTH = 1536
ROWS = 8 * TOK
BF16 = jnp.bfloat16
F32 = jnp.float32
I32 = jnp.int32
VMEM = pl.BlockSpec(memory_space=pltpu.VMEM)
HBM = pl.BlockSpec(memory_space=pltpu.HBM)
SMEM = pl.BlockSpec(memory_space=pltpu.SMEM)
MIB = 1 << 20


def permute(block, target):
    route = []
    for source in range(int(np.prod(FLAT))):
        goal = target(*(int(v) for v in np.unravel_index(source, FLAT)))
        if goal is not None:
            route.append((source, int(np.ravel_multi_index(goal, FLAT))))
    return lax.ppermute(block, AXES, route)


def swap_core(block):
    return permute(block, lambda y, zl, zh, x, c: (y, zl, zh, x, 1 - c))


def swap_half(block):
    return permute(block, lambda y, zl, zh, x, c: (y, zl, 1 - zh, x, c))


def swap_near(block, step):
    return permute(block, lambda y, zl, zh, x, c: (y, zl ^ step, zh, x, c))


def in_pair(mine, theirs, place):
    first = jnp.where(place == 0, mine, theirs)
    return jnp.concatenate([first, jnp.where(place == 0, theirs, mine)], axis=0)


def next_group(block):
    def target(y, zl, zh, x, c):
        if zl < 7:
            return (y, zl + 1, 0, x, c) if zh == 0 else None
        return (y + 1, 0, 0, x, c) if zh == 1 and y < 3 else None

    return permute(block, target)


def give_half(block, near):
    def target(y, zl, zh, x, c):
        return (y, zl, zh, x, 1 - c) if (c == zh) != near else None

    return permute(block, target)


def gather(block, axis):
    wide = jnp.broadcast_to(block[None], (lax.axis_size(axis),) + block.shape)
    return lax.all_to_all(wide, axis, split_axis=0, concat_axis=0, tiled=True)


def after(value, *earlier):
    return lax.optimization_barrier((value,) + earlier)[0]


def call(kernel, outs, in_specs, scratch=(), flops=0, nbytes=0, limit=16):
    outs = [jax.ShapeDtypeStruct(shape, kind) for shape, kind in outs]
    return pl.pallas_call(
        kernel,
        out_shape=outs,
        in_specs=in_specs,
        out_specs=[VMEM] * len(outs),
        scratch_shapes=list(scratch),
        compiler_params=pltpu.CompilerParams(vmem_limit_bytes=limit * MIB),
        cost_estimate=pl.CostEstimate(flops=flops, bytes_accessed=nbytes, transcendentals=0),
    )


def dot_nt(left, right):
    return lax.dot_general(left, right, (((1,), (1,)), ((), ())), preferred_element_type=F32)


def dot_tn(left, right):
    return lax.dot_general(left, right, (((0,), (0,)), ((), ())), preferred_element_type=F32)


def column(lane_row):
    return jnp.transpose(jnp.broadcast_to(lane_row, (TOK, TOK)))


def rms(values, gain):
    inverse = lax.rsqrt(jnp.mean(values * values, axis=-1, keepdims=True) + 1e-05)
    return (values * inverse * gain).astype(BF16)


def pack_kernel(meta, tokens, seg, ids, out):
    own = meta[5] * TOK + lax.broadcasted_iota(I32, (1, TOK), 1)
    back = own - seg[...]
    row = lax.broadcasted_iota(I32, (16, TOK), 0)
    pieces = jnp.where(row == 0, back >> 5, jnp.where(row == 1, back & 31, 0))
    pieces = jnp.where(row == 2, ids[0:1], jnp.where(row == 3, ids[1:2], pieces))
    pieces = pieces.astype(F32).astype(BF16)
    for copy in range(4):
        out[copy, :TOK] = tokens[...]
        out[copy, TOK:, :TOK] = pieces
        out[copy, TOK:, TOK:] = jnp.zeros((16, WIDTH - TOK), BF16)


def piece_kernel(meta, wq, wkv, wo, gate, up, down, out, sems):
    y = meta[0]
    place = lax.rem(meta[1], 4)
    piece = y * 4 + lax.rem(place, 2) * 2 + place // 2
    small = pl.ds(pl.multiple_of(y * 16, 16), 16)
    deep = pl.ds(pl.multiple_of(piece * 16, 16), 16)
    pairs = [
        (wq.at[small], out.at[0:16]),
        (wkv.at[small], out.at[16:32]),
        (wo.at[small], out.at[32:48]),
    ]
    for i in range(2):
        wide = pl.ds(pl.multiple_of(piece * 96 + 48 * i, 16), 48)
        pairs.append((gate.at[wide], out.at[48:96, 512 * i : 512 * i + 256]))
        pairs.append((up.at[wide], out.at[48:96, 512 * i + 256 : 512 * i + 512]))
    for i in range(3):
        chunk = slice(512 * i, 512 * i + 512)
        pairs.append((down.at[deep, chunk], out.at[48 + 16 * i : 64 + 16 * i, 1024:]))
    copies = [pltpu.make_async_copy(a, b, sems.at[n]) for n, (a, b) in enumerate(pairs)]
    for copy in copies:
        copy.start()
    for copy in copies:
        copy.wait()


def order_kernel(gate, up, down, out):
    for e in range(16):
        rows = slice(48 * e, 48 * e + 48)
        for i in range(2):
            low = 96 * e + 48 * i
            out[rows, 512 * i : 512 * i + 256] = gate[low : low + 48]
            out[rows, 512 * i + 256 : 512 * i + 512] = up[low : low + 48]
        for i in range(3):
            low = 48 * e + 16 * i
            out[low : low + 16, 1024:] = down[16 * e : 16 * e + 16, 512 * i : 512 * i + 512]


def project_kernel(meta, near, across, wq, wkv, wo, parts, gain,
                   q_out, kv_out, start_out, wo_out, cols):
    zh, c = meta[2], meta[4]
    cols[0:64] = wq[...]
    cols[pl.ds(pl.multiple_of(128 + zh * 64, 64), 64), :] = wkv[...]
    wo_out[0:64] = wo[...]
    for i in range(4):
        cols[64 + 16 * i : 80 + 16 * i] = parts[i, 0:16]
        cols[pl.ds(pl.multiple_of(192 - zh * 64 + 16 * i, 16), 16), :] = parts[i, 16:32]
        wo_out[64 + 16 * i : 80 + 16 * i] = parts[i, 32:48]
    for k in range(4):
        for block, core in ((near, c), (across, 1 - c)):
            low = pl.multiple_of((2 * k + core) * TOK, TOK)
            normed = rms(block[k, :TOK].astype(F32), gain[...])
            result = dot_nt(normed, cols[...]).astype(BF16)
            q_out[pl.ds(low, TOK), :] = result[:, :128]
            kv_out[pl.ds(low, TOK), :] = result[:, 128:]
            pieces = block[k, TOK:, :TOK].astype(F32)
            back = column(pieces[0:1] * 32.0 + pieces[1:2])
            own = (low + lax.broadcasted_iota(I32, (TOK, TOK), 0)).astype(F32)
            start_out[pl.ds(low, TOK), :] = own - back


def route_kernel(meta, near, across, pick_out, other_out, rows_out):
    x, c = meta[3], meta[4]
    before = lax.broadcasted_iota(I32, (TOK, TOK), 0) < lax.broadcasted_iota(I32, (TOK, TOK), 1)
    before = before.astype(F32).astype(BF16)
    row = lax.broadcasted_iota(I32, (CAP, TOK), 0).astype(F32)
    for expert, out in ((x + 4 * c, pick_out), (x + 4 * (1 - c), other_out)):
        number = expert.astype(F32)
        for k in range(4):
            for block, core in ((near, c), (across, 1 - c)):
                low = pl.multiple_of((2 * k + core) * CAP, 16)
                pieces = block[k, TOK:, :TOK].astype(F32)
                named = (pieces == number).astype(F32)
                named = named[2:3] + named[3:4]
                rank = jnp.dot(
                    jnp.broadcast_to(named, (8, TOK)).astype(BF16),
                    before,
                    preferred_element_type=F32,
                )[0:1]
                pick = jnp.where((row == rank) & (named > 0.0), 1.0, 0.0).astype(BF16)
                out[pl.ds(low, CAP), :] = pick
                if out is pick_out:
                    chosen = jnp.dot(pick, block[k, :TOK], preferred_element_type=F32)
                    rows_out[pl.ds(low, CAP), :] = chosen.astype(BF16)


def split_kv(kv):
    wide = kv[...].astype(F32)
    turned = pltpu.roll(wide, 64, 1)
    low = lax.broadcasted_iota(I32, wide.shape, 1) < 64
    return (
        jnp.where(low, wide, turned).astype(BF16),
        jnp.where(low, turned, wide).astype(BF16),
    )


STEP = 256


def own_kernel(q, kv, start, ids, sum_out, stat_out, slots_out, keys, values):
    keys[...], values[...] = split_kv(kv)
    low_lane = lax.broadcasted_iota(I32, (STEP, 128), 1) < 64
    for block in range(ROWS // STEP):
        low = block * STEP
        span = low + STEP
        query = q[low:span]
        position = lax.broadcasted_iota(I32, (STEP, span), 1).astype(F32)
        own = (low + lax.broadcasted_iota(I32, (STEP, span), 0)).astype(F32)
        allowed = (position <= own) & (position >= start[low:span, 0:1])
        parts = []
        for head in range(2):
            kept = jnp.where(low_lane if head == 0 else ~low_lane, query, jnp.zeros_like(query))
            scores = jnp.where(allowed, dot_nt(kept, keys[:span]) * 0.125, -1e30)
            top = jnp.max(scores, axis=-1, keepdims=True)
            weights = jnp.exp(scores - top)
            den = jnp.sum(weights, axis=-1, keepdims=True)
            part = jnp.dot(weights.astype(BF16), values[:span], preferred_element_type=F32)
            parts.append((part, top, den))
        sum_out[low:span] = jnp.where(low_lane, parts[0][0], parts[1][0])
        lane = lax.broadcasted_iota(I32, (STEP, 128), 1)
        stats = jnp.where(lane == 0, start[low:span, 0:1], parts[0][1])
        for n, column_of in ((2, parts[1][1]), (3, parts[0][2]), (4, parts[1][2])):
            stats = jnp.where(lane == n, column_of, stats)
        stat_out[low:span] = stats
    choice = [ids[k : k + 1].astype(F32) for k in range(2)]
    down = [column(v) for v in choice]
    earlier = lax.broadcasted_iota(I32, (TOK, TOK), 0) < lax.broadcasted_iota(I32, (TOK, TOK), 1)
    result = []
    for k in range(2):
        same = sum((down[j] == choice[k]).astype(F32) for j in range(2))
        rank = jnp.sum(jnp.where(earlier, same, 0.0), axis=0, keepdims=True).astype(I32)
        expert = ids[k : k + 1]
        result.append(((expert & 3) * 2 + (expert >> 2)) * CAP + rank)
    row = lax.broadcasted_iota(I32, (8, TOK), 0)
    slots_out[...] = jnp.where(row == 0, result[0], result[1])


def before_kernel(q, kv, sums, stats, pages, out, keys, values):
    keys[...], values[...] = split_kv(kv)
    low_lane = lax.broadcasted_iota(I32, (STEP, 128), 1) < 64
    for block in range(ROWS // STEP):
        low = block * STEP
        high = low + STEP
        span = ROWS - low
        query = q[low:high]
        position = (low - ROWS + lax.broadcasted_iota(I32, (STEP, span), 1)).astype(F32)
        allowed = position >= stats[low:high, 0:1]
        parts = []
        for head in range(2):
            kept = jnp.where(low_lane if head == 0 else ~low_lane, query, jnp.zeros_like(query))
            scores = jnp.where(allowed, dot_nt(kept, keys[low:]) * 0.125, -1e30)
            first = stats[low:high, 1 + head : 2 + head]
            top = jnp.maximum(first, jnp.max(scores, axis=-1, keepdims=True))
            weights = jnp.exp(scores - top)
            scale = jnp.exp(first - top)
            den = jnp.sum(weights, axis=-1, keepdims=True)
            den += stats[low:high, 3 + head : 4 + head] * scale
            part = jnp.dot(weights.astype(BF16), values[low:], preferred_element_type=F32)
            parts.append((part, scale, den))
        part, scale, den = (jnp.where(low_lane, one, two) for one, two in zip(*parts))
        total = sums[low:high] * scale + part
        result = (total / den).astype(BF16)
        for copy in range(4):
            out[copy, low:high, :] = result
    for k in range(4):
        out[k, ROWS:, :] = pages[k * 256 : k * 256 + 256]


def page_kernel(meta, table, kv, partner, out, group):
    zh = meta[2]
    group[pl.ds(pl.multiple_of(zh * ROWS, ROWS), ROWS), :] = kv[...]
    group[pl.ds(pl.multiple_of((1 - zh) * ROWS, ROWS), ROWS), :] = partner[...]

    def place(block, carry):
        page = table[0, block] - zh * 64

        @pl.when((page >= 0) & (page < 64))
        def _():
            out[pl.ds(pl.multiple_of(page * PAGE, PAGE), PAGE), :] = group[
                pl.ds(pl.multiple_of(block * PAGE, PAGE), PAGE), :
            ]

        return carry

    lax.fori_loop(0, 128, place, 0)


def cache_kernel(meta, keep, got, out):
    c = meta[4]
    low = lax.broadcasted_iota(I32, (TOK, 128), 1) < 64
    for pair in range(4):
        lanes = slice(pair * 128, pair * 128 + 128)
        mine = keep[4 * TOK :, lanes].astype(F32)
        theirs = got[4 * TOK :, lanes].astype(F32)
        one = jnp.where(c == 0, mine, theirs)
        two = jnp.where(c == 0, theirs, mine)
        out[:, lanes] = jnp.where(low, one, pltpu.roll(two, 64, 1)).astype(BF16)
        lanes = slice(512 + pair * 128, 640 + pair * 128)
        out[:, lanes] = jnp.where(low, pltpu.roll(one, 64, 1), two).astype(BF16)


def choose(slots, k):
    place = lax.broadcasted_iota(I32, (8 * CAP, TOK), 0)
    return place == slots[k : k + 1]


def split_kernel(meta, heads, pick, other, keep_out, give_out):
    x, c = meta[3], meta[4]
    for d in range(8):
        rows = jnp.concatenate([heads[k, d * TOK : d * TOK + TOK] for k in range(4)], axis=1)
        low = slice(d * CAP, d * CAP + CAP)
        keep_out[low] = jnp.dot(pick[low], rows, preferred_element_type=F32).astype(BF16)
        give_out[low] = jnp.dot(other[low], rows, preferred_element_type=F32).astype(BF16)
    for out, core in ((keep_out, c), (give_out, 1 - c)):
        low = pl.multiple_of((2 * x + core) * TOK, TOK)
        page = pl.multiple_of(ROWS + core * TOK, TOK)
        for k in range(4):
            lanes = slice(k * 128, k * 128 + 128)
            out[8 * CAP : 4 * TOK, lanes] = heads[k, pl.ds(low, TOK), :]
            out[4 * TOK :, lanes] = heads[k, pl.ds(page, TOK), :]


def expert_kernel(meta, keep, got, wo_all, rows, tokens, gain, own, other, given_a, given_b,
                  mid_out, out, raw, wide, deep, sems):
    zh, c = meta[2], meta[4]

    @pl.when(c == zh)
    def _():
        pltpu.make_async_copy(own, raw.at[0], sems.at[0]).start()
        pltpu.make_async_copy(given_a, raw.at[1], sems.at[1]).start()

    @pl.when(c != zh)
    def _():
        pltpu.make_async_copy(other, raw.at[0], sems.at[0]).start()
        pltpu.make_async_copy(given_b, raw.at[1], sems.at[1]).start()

    tiles = []
    for k in range(4):
        one = keep[: 4 * TOK, k * 128 : k * 128 + 128]
        two = got[: 4 * TOK, k * 128 : k * 128 + 128]
        tiles += [jnp.where(c == 0, one, two), jnp.where(c == 0, two, one)]
    total = jnp.dot(jnp.concatenate(tiles, axis=1), wo_all[...], preferred_element_type=F32)
    mid_out[...] = (tokens[...].astype(F32) + total[8 * CAP :]).astype(BF16)
    mid = (rows[...].astype(F32) + total[: 8 * CAP]).astype(BF16)
    arrived = rms(mid.astype(F32), gain[...])
    acts = []
    for half, source in enumerate((own, given_a)):
        pltpu.make_async_copy(source, raw.at[half], sems.at[half]).wait()
        for e in range(16):
            for i in range(2):
                low = 96 * e + 48 * i
                wide[half, low : low + 48] = raw[
                    half, 48 * e : 48 * e + 48, 512 * i : 512 * i + 512
                ]
            for i in range(3):
                low = 48 * e + 16 * i
                deep[half, i * 256 + e * 16 : i * 256 + e * 16 + 16] = raw[
                    half, low : low + 16, 1024:
                ]
        both = jnp.dot(arrived, wide[half], preferred_element_type=F32)
        gate, up = both[:, :256], both[:, 256:]
        acts.append((gate / (1.0 + jnp.exp(-gate)) * up).astype(BF16))
    for i in range(3):
        chunk = slice(i * 256, i * 256 + 256)
        total = jnp.dot(acts[0], deep[0, chunk], preferred_element_type=F32)
        total += jnp.dot(acts[1], deep[1, chunk], preferred_element_type=F32)
        out[:, i * 512 : i * 512 + 512] = total.astype(BF16)


def combine_kernel(returned, mid, slots, weights, out):
    total = mid[...].astype(F32)
    for k in range(2):
        pick = choose(slots, k).astype(F32).astype(BF16)
        chosen = dot_tn(pick, returned[...])
        total += chosen * column(weights[k : k + 1])[:, 0:1]
    out[...] = total.astype(BF16)


def body(
    tokens,
    attn_gain,
    ffn_gain,
    w_query,
    key_value_weight,
    w_out,
    segment_ids,
    expert_ids,
    route_weights,
    w_gate,
    w_up,
    w_down,
    page_table,
):
    y, zq, zr, zp, zh, x, c = (lax.axis_index(name) for name in AXES)
    zl = zq * 4 + zr * 2 + zp
    place = (((y * 8 + zl) * 2 + zh) * 4 + x) * 2 + c
    meta = jnp.stack([y, zl, zh, x, c, place]).astype(I32)
    wq, wkv = w_query.T, key_value_weight.T
    ids = expert_ids.T

    (block,) = call(
        pack_kernel, [((4, TOK + 16, WIDTH), BF16)], [SMEM] + [VMEM] * 3, nbytes=0
    )(meta, tokens, segment_ids[None, :], ids)
    (piece,) = call(
        piece_kernel,
        [((96, WIDTH), BF16)],
        [SMEM] + [HBM] * 6,
        scratch=[pltpu.SemaphoreType.DMA((10,))],
        limit=60,
    )(meta, wq, wkv, w_out, w_gate, w_up, w_down)
    near = lax.all_to_all(block, "x", split_axis=0, concat_axis=0, tiled=True)
    near, piece = lax.optimization_barrier((near, swap_half(piece)))
    parts = gather(piece[:48], "y")
    across = swap_core(near)
    beside = swap_near(piece[48:], 2)
    gain, beside = lax.optimization_barrier((attn_gain[None, :], beside))
    q, kv, start, out_rows = call(
        project_kernel,
        [((ROWS, 128), BF16), ((ROWS, 128), BF16), ((ROWS, 128), F32), ((128, WIDTH), BF16)],
        [SMEM] + [VMEM] * 7,
        scratch=[pltpu.VMEM((256, WIDTH), BF16)],
    )(meta, near, across, wq, wkv, w_out, parts, gain)
    out_all = lax.all_gather(out_rows, ROW, axis=0, tiled=True)

    partner = swap_half(kv)
    sums, stats, slots = call(
        own_kernel,
        [((ROWS, 128), F32)] * 2 + [((8, TOK), I32)],
        [VMEM] * 4,
        scratch=[pltpu.VMEM((ROWS, 128), BF16)] * 2,
        flops=4000000000,
        nbytes=3000000,
    )(q, kv, start, ids)
    pick, other_pick, chosen = call(
        route_kernel,
        [((8 * CAP, TOK), BF16)] * 2 + [((8 * CAP, WIDTH), BF16)],
        [SMEM] + [VMEM] * 2,
        flops=2000000000,
        nbytes=5000000,
    )(meta, after(near, kv), across)

    (own,) = call(order_kernel, [((768, WIDTH), BF16)], [VMEM] * 3, nbytes=5000000)(
        *(after(w, kv) for w in (w_gate, w_up, w_down))
    )
    pair = in_pair(after(piece[48:], kv), after(beside, kv), zr)
    four = in_pair(pair, swap_near(pair, 1), zp)
    partner, sums, pick, own, four, out_all = lax.optimization_barrier(
        (partner, sums, pick, own, four, out_all)
    )
    onward = jnp.where(zh == 0, partner, kv)
    shifted = next_group(onward)
    given_a = give_half(own, True)
    other = lax.all_gather(four, "y", axis=0, tiled=True)
    (pages,) = call(
        page_kernel,
        [((ROWS, 128), BF16)],
        [SMEM, SMEM] + [VMEM] * 2,
        scratch=[pltpu.VMEM((2 * ROWS, 128), BF16)],
        nbytes=0,
    )(meta, page_table, kv, partner)
    previous = jnp.where(zh == 0, shifted, partner)
    (heads,) = call(
        before_kernel,
        [((4, ROWS + 256, 128), BF16)],
        [VMEM] * 5,
        scratch=[pltpu.VMEM((ROWS, 128), BF16)] * 2,
        flops=0,
        nbytes=0,
        limit=60,
    )(q, previous, sums, stats, pages)
    heads = lax.all_to_all(heads, "x", split_axis=0, concat_axis=0, tiled=True)
    keep, give = call(
        split_kernel,
        [((5 * TOK, 512), BF16)] * 2,
        [SMEM] + [VMEM] * 3,
        flops=0,
        nbytes=0,
        limit=60,
    )(meta, heads, pick, other_pick)
    got = swap_core(give)
    other = after(other, give)
    given_b = give_half(other, False)
    mid, expert_out = call(
        expert_kernel,
        [((TOK, WIDTH), BF16), ((8 * CAP, WIDTH), BF16)],
        [SMEM] + [VMEM] * 6 + [HBM] * 4,
        scratch=[
            pltpu.VMEM((2, 768, WIDTH), BF16),
            pltpu.VMEM((2, WIDTH, 512), BF16),
            pltpu.VMEM((2, 768, 512), BF16),
            pltpu.SemaphoreType.DMA((2,)),
        ],
        limit=60,
        flops=0,
        nbytes=0,
    )(meta, keep, got, out_all, chosen, tokens, ffn_gain[None, :], own, other, given_a, given_b)
    (cache,) = call(cache_kernel, [((TOK, 1024), BF16)], [SMEM] + [VMEM] * 2, nbytes=800000)(
        meta, after(keep, expert_out), got
    )
    returned = lax.all_to_all(
        expert_out.reshape(8, CAP, WIDTH), ROW, split_axis=0, concat_axis=0, tiled=True
    ).reshape(8 * CAP, WIDTH)
    (hidden,) = call(
        combine_kernel, [((TOK, WIDTH), BF16)], [VMEM] * 4, flops=0, nbytes=0
    )(returned, mid, slots, route_weights.T)
    return (hidden, cache.reshape(8, PAGE, 1024))


def solution(mesh):
    fine = Mesh(mesh.devices.reshape(SIZES), AXES)
    grp, tp = ("y", "zq", "zr", "zp"), ("zh", "x", "c")
    in_specs = (
        P(AXES, None),
        P(),
        P(),
        P(None, tp),
        P(None, tp),
        P(tp, None),
        P(AXES),
        P(AXES, None),
        P(AXES, None),
        P(None, tp),
        P(None, tp),
        P(tp, None),
        P(grp, None),
    )
    out_specs = (P(AXES, None), P(AXES, None, None))
    return jax.shard_map(body, mesh=fine, in_specs=in_specs, out_specs=out_specs, check_vma=False)
```
